128 devices in a mesh: genome: 64 (over z, y, x), sample: 2 (over core).
Axes of the slice: x: 4, y: 4, z: 4, core: 2. Of those that a mesh axis runs over, the one named last changes fastest.
Arguments:
- genotypes: bfloat16 [32768, 8192], P('genome', 'sample'), may hold values from 0.049804688 to 2
- phenotypes: bfloat16 [4096, 8192], P('genome', 'sample'), may hold values from -60 to 60
- environment: float32 [8192], P('sample'), may hold values from 0.3 to 3
- shuffles: int32 [4, 8192], P(None, 'sample'), may hold values from 0 to 8191, each once within a row
- window_start: int32 [4096], replicated, may hold values from 0 to 127, as said below
- window_end: int32 [4096], replicated, may hold values from 1 to 128, as said below
- chrom_bounds: int32 [21], replicated, may hold values from 1 to 127, as said below
Outputs:
- maxima: float32 [5, 4096], P(None, 'genome')
The draws below stay inside these ranges and needn't reach their ends.
Inputs may be any that keep to these rules, and one draw needn't show every extreme that they name: `window_start`: for gene g on genome index d = g // 64 the window is [c - l, c + r + 1) cut to [0, 128), where d * 2 <= c < (d + 1) * 2 and 1 <= l, r <= 7; the first gene of every index has c = d * 2 and l = 7, the last has c = (d + 1) * 2 - 1 and r = 7. `window_end`: the end of the window described for window_start. `chrom_bounds`: strictly increasing.
All inputs are finite; a program needn't handle non-finite values.
Results may differ from the reference program's by a relative error of at most 0.0024.
Values may be sent and summed in bfloat16 or wider, within the bound.
A program may use at most 128 MiB of HBM per device.

```python
import math
import jax
import jax.numpy as jnp
from jax import lax

SNP_BLOCK = 256
SNP_DEV = 512
GENE_DEV = 64
PERMS = 4
HALF_BLK = 7
P1 = 5
BLK_DEV = 2
REACH = 4
BAND = 9
SNPS = 32768
GENES = 4096
SAMPLES = 8192
NBLK = 128
CHROMS = 22
N_GENOME = 64


def window_pair(key):
    center_key, left_key, right_key = jax.random.split(jax.random.fold_in(key, 11), 3)
    genes = jnp.arange(GENES, dtype=jnp.int32)
    owner = genes // GENE_DEV
    within = genes % GENE_DEV
    shifted = jax.random.randint(center_key, (GENES,), 0, BLK_DEV, dtype=jnp.int32)
    shifted = jnp.where(within == 0, 0, jnp.where(within == GENE_DEV - 1, BLK_DEV - 1, shifted))
    center = owner * BLK_DEV + shifted
    left_reach = jax.random.randint(left_key, (GENES,), 1, HALF_BLK + 1, dtype=jnp.int32)
    right_reach = jax.random.randint(right_key, (GENES,), 1, HALF_BLK + 1, dtype=jnp.int32)
    left_reach = jnp.where(within == 0, HALF_BLK, left_reach)
    right_reach = jnp.where(within == GENE_DEV - 1, HALF_BLK, right_reach)
    starts = jnp.maximum(center - left_reach, 0)
    ends = jnp.minimum(center + right_reach + 1, NBLK)
    return (starts, ends)


def draw_window_start(key, part):
    return window_pair(key)[0]


def draw_window_end(key, part):
    return window_pair(key)[1]


def draw_chrom_bounds(key, part):
    order = jax.random.permutation(jax.random.fold_in(key, 5), NBLK - 1) + 1
    return jnp.sort(order[:CHROMS - 1]).astype(jnp.int32)


def draw_phenotypes(key, part):
    base_key, column_key = jax.random.split(jax.random.fold_in(key, 3), 2)
    base = jax.random.normal(base_key, (GENES, SAMPLES), jnp.float32)
    column_scale = jnp.exp(jax.random.uniform(column_key, (1, SAMPLES), jnp.float32, math.log(0.3), math.log(3.0)))
    values = base * column_scale
    return jnp.clip(values, -60.0, 60.0).astype(jnp.bfloat16)


def level_of(key, dims, pieces, low, top_value):
    def one(axis_at, blocks):
        steps = jax.random.uniform(jax.random.fold_in(jax.random.fold_in(key, 6), axis_at), (blocks,), jnp.float32, low / len(pieces), top_value / len(pieces))
        return jnp.repeat(jnp.exp(steps), dims[axis_at] // blocks).reshape((-1,) + (1,) * (len(dims) - axis_at - 1))

    gain = one(*pieces[0])
    for cut in pieces[1:]:
        gain = gain * one(*cut)
    return gain


def setup_inputs(seed: int = 0) -> dict:
    streams_of = jax.random.split(jax.random.key(seed), 8)
    return {
        "genotypes": jnp.clip(0.049804688 + 1.9501953 * jax.random.uniform(streams_of[0], (SNPS, SAMPLES), jnp.float32) ** level_of(streams_of[0], (SNPS, SAMPLES), ((0, 64), (1, 2)), -0.2, 0.2), 0.049804688, 2.0).astype(jnp.bfloat16),
        "phenotypes": draw_phenotypes(jax.random.fold_in(streams_of[7], 71), 0),
        "environment": jnp.clip(jnp.exp(math.log(3.0) - 2.3025851 * jax.random.uniform(streams_of[2], (SAMPLES,), jnp.float32) ** level_of(streams_of[2], (SAMPLES,), ((0, 2),), -0.2, 0.2)), 0.3, 3.0),
        "shuffles": jax.vmap(lambda own: jax.random.permutation(own, SAMPLES))(jax.random.split(streams_of[3], PERMS)).reshape((PERMS, SAMPLES)).astype(jnp.int32),
        "window_start": draw_window_start(jax.random.fold_in(streams_of[7], 71), 0),
        "window_end": draw_window_end(jax.random.fold_in(streams_of[7], 71), 0),
        "chrom_bounds": draw_chrom_bounds(jax.random.fold_in(streams_of[7], 71), 0),
    }


def window_bounds(window_start, window_end, chrom_bounds, total_blocks):
    middle = (window_start + window_end - 1) // 2
    before = chrom_bounds[None, :] <= middle[:, None]
    lower_edge = lax.optimization_barrier(jnp.max(jnp.where(before, chrom_bounds[None, :], 0), axis=1))
    upper_edge = lax.optimization_barrier(jnp.min(jnp.where(before, total_blocks, chrom_bounds[None, :]), axis=1))
    return (jnp.maximum(window_start, lower_edge), jnp.minimum(window_end, upper_edge))

def window_scores(reduced, square_sum, cross_sum, inter_sum):
    half_cols = reduced.shape[1] // 2
    marginal = reduced[:, :half_cols]
    interact = reduced[:, half_cols:]
    regression = cross_sum / square_sum
    resid_norm = inter_sum - cross_sum * regression
    divisor = resid_norm + 0.1 * inter_sum
    numerator = interact - regression[:, None] * marginal
    return numerator * numerator / divisor[:, None]

def reference(genotypes, phenotypes, environment, shuffles, window_start, window_end, chrom_bounds):
    lower_edge, upper_edge = window_bounds(window_start, window_end, chrom_bounds, NBLK)
    geno_float = genotypes.astype(jnp.float32)
    squares = geno_float * geno_float
    square_sum = lax.optimization_barrier(jnp.sum(squares, axis=1))
    cross_sum = lax.optimization_barrier(jnp.sum(squares * environment[None, :], axis=1))
    inter_sum = lax.optimization_barrier(jnp.sum(squares * (environment * environment)[None, :], axis=1))
    margin_rows = REACH * SNP_DEV
    pad_square = jnp.full((margin_rows,), 1.0, jnp.float32) * SAMPLES
    pad_cross = jnp.full((margin_rows,), 1.0, jnp.float32) * jnp.sum(environment)
    pad_inter = jnp.full((margin_rows,), 1.0, jnp.float32) * jnp.sum(environment * environment)
    square_pad = jnp.concatenate([pad_square, square_sum, pad_square])
    cross_pad = jnp.concatenate([pad_cross, cross_sum, pad_cross])
    inter_pad = jnp.concatenate([pad_inter, inter_sum, pad_inter])
    ones_rows = jnp.ones((margin_rows, SAMPLES), jnp.bfloat16)
    padded_geno = jnp.concatenate([ones_rows, genotypes, ones_rows], axis=0)
    row_power = lax.optimization_barrier(jnp.sum(jnp.square(phenotypes.astype(jnp.float32)), axis=1))

    def gene_block(block_index):
        gene_slab = lax.dynamic_slice_in_dim(phenotypes, block_index * GENE_DEV, GENE_DEV, 0)
        shuffled = jnp.take(gene_slab, shuffles, axis=1)
        stacked = jnp.concatenate([gene_slab[None], jnp.transpose(shuffled, (1, 0, 2))], axis=0)
        stacked = stacked.reshape(P1 * GENE_DEV, SAMPLES)
        weighted = (stacked.astype(jnp.float32) * environment[None, :]).astype(jnp.bfloat16)
        operand = jnp.concatenate([stacked, weighted], axis=0)
        first_row = block_index * SNP_DEV
        geno_slab = lax.dynamic_slice_in_dim(padded_geno, first_row, BAND * SNP_DEV, 0)
        reduced = lax.dot_general(geno_slab, operand, (((1,), (1,)), ((), ())), preferred_element_type=jnp.float32)
        scores = window_scores(reduced, lax.dynamic_slice_in_dim(square_pad, first_row, BAND * SNP_DEV, 0), lax.dynamic_slice_in_dim(cross_pad, first_row, BAND * SNP_DEV, 0), lax.dynamic_slice_in_dim(inter_pad, first_row, BAND * SNP_DEV, 0)).reshape(BAND * SNP_DEV, P1, GENE_DEV)
        row_blocks = ((block_index - REACH) * SNP_DEV + jnp.arange(BAND * SNP_DEV, dtype=jnp.int32)) // SNP_BLOCK
        lower_band = lax.dynamic_slice_in_dim(lower_edge, block_index * GENE_DEV, GENE_DEV, 0)
        upper_band = lax.dynamic_slice_in_dim(upper_edge, block_index * GENE_DEV, GENE_DEV, 0)
        inside = (row_blocks[:, None] >= lower_band[None, :]) & (row_blocks[:, None] < upper_band[None, :])
        best_peak = lax.optimization_barrier(jnp.max(jnp.where(inside[:, None, :], scores, 0.0), axis=0))
        power_band = lax.dynamic_slice_in_dim(row_power, block_index * GENE_DEV, GENE_DEV, 0)
        return jnp.sqrt(best_peak / (power_band[None, :] / SAMPLES + 1e-05))
    blocks_out = lax.map(gene_block, jnp.arange(N_GENOME, dtype=jnp.int32))
    return jnp.transpose(blocks_out, (1, 0, 2)).reshape(P1, GENES)
```

```python
import functools

import jax
import jax.numpy as jnp
from jax import lax
from jax.experimental import pallas as pl
from jax.experimental.pallas import tpu as pltpu
from jax.sharding import PartitionSpec as P

SNP_BLOCK = 256
MESH = pl.DeviceIdType.MESH
NEAR = (-4, -1, 0, 1, 4)
FAR = (-3, -2, 2, 3)
SLOTS = NEAR + FAR
CORE_SLOTS = (NEAR[:4] + FAR, NEAR[1:] + FAR)
STEP = 512
FAR_STEP = 1024


def window_bounds(window_start, window_end, chrom_bounds, total_blocks):
    middle = (window_start + window_end - 1) // 2
    before = chrom_bounds[None, :] <= middle[:, None]
    lower_edge = jnp.max(jnp.where(before, chrom_bounds[None, :], 0), axis=1)
    upper_edge = jnp.min(jnp.where(before, total_blocks, chrom_bounds[None, :]), axis=1)
    return (jnp.maximum(window_start, lower_edge), jnp.minimum(window_end, upper_edge))


def when(condition, action):
    if condition is None:
        action()
    else:
        pl.when(condition)(action)


def inverse_kernel(own_ref, other_ref, out_ref):
    core = lax.axis_index("sample")
    perms, half = own_ref.shape
    width = 2048
    rows = half // 128
    for p in range(perms):
        total = jnp.zeros((2 * rows, 128), jnp.float32)
        for part, ref in enumerate((own_ref, other_ref)):
            for start in range(0, half, width):
                target = ref[p : p + 1, start : start + width]
                high = (target >> 7) - rows * core
                low = target & 127
                place = lax.broadcasted_iota(jnp.int32, (1, width), 1) + (part * half + start)
                hit = lax.broadcasted_iota(jnp.int32, (rows, width), 0) == high
                place_high = (place >> 7).astype(jnp.float32)
                place_low = (place & 127).astype(jnp.float32)
                left = jnp.concatenate(
                    [jnp.where(hit, place_high, 0.0), jnp.where(hit, place_low, 0.0)], axis=0
                ).astype(jnp.bfloat16)
                right = jnp.where(
                    lax.broadcasted_iota(jnp.int32, (128, width), 0) == low, 1.0, 0.0
                ).astype(jnp.bfloat16)
                total += lax.dot_general(
                    left, right, (((1,), (1,)), ((), ())), preferred_element_type=jnp.float32
                )
        out_ref[p * rows : (p + 1) * rows, :] = (
            total[:rows] * 128.0 + total[rows:]
        ).astype(jnp.int32)


def scan_kernel(
    inv_ref, y_ref, g_ref, env_ref, mask_ref, out_ref,
    h_ref, gp_ref, band_ref, other_ref, env_other, mom_ref, mom_other, reg_ref, div_ref,
    stage0, stage1, near_acc, far_acc, near_in, far_in, peak_ref, msg_ref, msg_in, pow_ref, pow_other,
    y_send, y_recv, g_send, g_recv, s_send, s_recv, p_send, p_recv, m_send, m_recv, local_sem,
):
    me = lax.axis_index("genome")
    core = lax.axis_index("sample")
    indices = lax.axis_size("genome")
    sib = (me, 1 - core)
    genes, half = y_ref.shape
    snps = g_ref.shape[0]

    def inside(o):
        return (me + o >= 0) & (me + o < indices)

    barrier = pltpu.get_barrier_semaphore()
    pl.semaphore_signal(barrier, inc=1, device_id=sib, device_id_type=MESH)
    count = jnp.int32(1)
    for o in SLOTS:
        if o != 0:
            for k in range(2):
                @pl.when(inside(o))
                def _(o=o, k=k):
                    pl.semaphore_signal(barrier, inc=1, device_id=(me + o, k), device_id_type=MESH)
            count = count + jnp.where(inside(o), 2, 0)
    pl.semaphore_wait(barrier, count)

    def remote(src, dst, send, recv, target):
        return pltpu.make_async_remote_copy(
            src, dst, send, recv, device_id=target, device_id_type=MESH
        )

    width = half // 4
    g_copies = [
        remote(
            g_ref.at[:, pl.ds(i * width, width)], other_ref.at[:, pl.ds(i * width, width)],
            g_send.at[i], g_recv.at[i], sib,
        )
        for i in range(4)
    ]
    env_copy = remote(env_ref, env_other, s_send.at[0], s_recv.at[0], sib)
    y_copies = []
    for slot, o in enumerate(SLOTS):
        if o != 0:
            i = len(y_copies)
            y_copies.append((o, remote(
                y_ref, band_ref.at[pl.ds(slot * genes, genes), :], y_send.at[i], y_recv.at[i],
                (me - o, core),
            )))
    own_copy = pltpu.make_async_copy(y_ref, band_ref.at[pl.ds(2 * genes, genes), :], local_sem)
    own_copy.start()
    env_copy.start()
    for copy in g_copies:
        copy.start()
    for o, copy in y_copies:
        when(inside(-o), copy.start)

    lane = lax.broadcasted_iota(jnp.int32, (64, 128), 1)

    def moments(block, _):
        first = pl.multiple_of(block * 64, 64)
        square = jnp.zeros((64, 128), jnp.float32)
        cross = square
        inter = square
        for column in range(half // 128):
            value = g_ref[pl.ds(first, 64), column * 128 : (column + 1) * 128].astype(jnp.float32)
            weight = env_ref[column : column + 1, :]
            value = value * value
            once = value * weight
            square += value
            cross += once
            inter += once * weight
        square = jnp.sum(square, axis=1, keepdims=True)
        cross = jnp.sum(cross, axis=1, keepdims=True)
        inter = jnp.sum(inter, axis=1, keepdims=True)
        mom_ref[pl.ds(first, 64), :] = jnp.where(lane == 0, square, jnp.where(lane == 1, cross, inter))
        return 0

    lax.fori_loop(0, snps // 64, moments, 0)
    mom_copy = remote(mom_ref, mom_other, s_send.at[1], s_recv.at[1], sib)
    mom_copy.start()

    power = jnp.zeros((genes, 128), jnp.float32)
    for column in range(half // 128):
        value = y_ref[:, column * 128 : (column + 1) * 128].astype(jnp.float32)
        power += value * value
    power = jnp.broadcast_to(jnp.sum(power, axis=1, keepdims=True), (genes, 128))
    power = jnp.concatenate([power, power], axis=0)
    pow_ref[...] = jnp.transpose(power)[0:8, :]
    pow_copy = remote(pow_ref, pow_other, s_send.at[2], s_recv.at[2], sib)
    pow_copy.start()

    near_acc[...] = jnp.zeros_like(near_acc)
    far_acc[...] = jnp.zeros_like(far_acc)
    mom_copy.wait_recv()
    env_copy.wait_recv()
    for q in range(4):
        rows = slice(q * 128, (q + 1) * 128)
        total = mom_ref[rows, :] + mom_other[rows, :]
        square, cross, inter = total[:, 0:1], total[:, 1:2], total[:, 2:3]
        regression = cross / square
        divisor = inter - cross * regression + 0.1 * inter
        reg_ref[rows, :] = jnp.broadcast_to(regression, (128, 128))
        div_ref[:, rows] = jnp.transpose(jnp.broadcast_to(divisor, (128, 128)))[0:8, :]

    def residuals(source, weights, first, chunk):
        for s in range(2):
            start = pl.multiple_of(chunk * 256 + s * 128, 128)
            weight = weights[pl.ds(chunk * 2 + s, 1), :]
            for q in range(4):
                rows = slice(q * 128, (q + 1) * 128)
                value = source[rows, pl.ds(start, 128)].astype(jnp.float32)
                value = jnp.transpose(value * (weight - reg_ref[rows, :]))
                h_ref[pl.ds(first + start, 128), q, :] = value

    def own_residuals(chunk, _):
        residuals(g_ref, env_ref, 0, chunk)
        return 0

    lax.fori_loop(0, half // 256, own_residuals, 0)
    own_copy.wait()
    for o, copy in y_copies:
        if o in NEAR:
            when(inside(o), copy.wait_recv)

    def right_side(ref, first, b, count):
        return jnp.concatenate(
            [ref[pl.ds(first, count), 2 * b + i, :] for i in range(2)], axis=1
        ).astype(jnp.bfloat16)

    def near_product(label, k, sides):
        for b in range(2):
            left = band_ref[64 * b : 64 * b + 256, pl.ds(pl.multiple_of(k * STEP, STEP), STEP)]
            near_acc[2 * label + b] += jnp.dot(left, sides[b], preferred_element_type=jnp.float32)

    def plain(k, _):
        near_product(0, k, [right_side(h_ref, pl.multiple_of(k * STEP, STEP), b, STEP) for b in range(2)])
        return 0

    lax.fori_loop(0, half // STEP, plain, 0)

    for i in range(4):
        g_copies[i].wait_recv()

        def other_residuals(chunk, _):
            residuals(other_ref, env_other, half, chunk)
            return 0

        lax.fori_loop(i * width // 256, (i + 1) * width // 256, other_residuals, 0)

    per_label = half // STEP
    steps = 4 * per_label

    def gather(stage, n):
        base = n * STEP
        for t in range(STEP):
            stage[t] = h_ref[inv_ref[base + t]]

    def consume(stage, n):
        sides = [right_side(stage, 0, b, STEP) for b in range(2)]
        for b in range(2):
            gp_ref[pl.ds(pl.multiple_of(n * STEP, STEP), STEP), 256 * b : 256 * b + 256] = sides[b]
        near_product(1 + lax.div(n, per_label), lax.rem(n, per_label), sides)

    def permuted(i, _):
        n = 2 * i
        gather(stage1, n + 1)
        consume(stage0, n)
        gather(stage0, lax.rem(n + 2, steps))
        consume(stage1, n + 1)
        return 0

    gather(stage0, 0)
    lax.fori_loop(0, steps // 2, permuted, 0)

    partials = []
    for label in range(5):
        copy = remote(
            near_acc.at[2 * label + 1 - core], near_in.at[label], p_send.at[label], p_recv.at[label], sib
        )
        copy.start()
        partials.append(copy)
    for o, copy in y_copies:
        if o in FAR:
            when(inside(o), copy.wait_recv)

    for label in range(5):
        def distant(k, _, label=label):
            start = pl.multiple_of(k * FAR_STEP, FAR_STEP)
            left = band_ref[320:576, pl.ds(start, FAR_STEP)]
            for b in range(2):
                if label == 0:
                    side = right_side(h_ref, start, b, FAR_STEP)
                else:
                    side = gp_ref[pl.ds(start + (label - 1) * half, FAR_STEP), 256 * b : 256 * b + 256]
                far_acc[2 * label + b] += jnp.dot(left, side, preferred_element_type=jnp.float32)
            return 0

        lax.fori_loop(0, half // FAR_STEP, distant, 0)
        copy = remote(
            far_acc.at[2 * label + 1 - core], far_in.at[label], p_send.at[5 + label], p_recv.at[5 + label], sib
        )
        copy.start()
        partials.append(copy)

    divisor = div_ref[0:1, pl.ds(pl.multiple_of(core * 256, 256), 256)]
    lanes = lax.broadcasted_iota(jnp.int32, (256, 128), 1)
    for part, (acc, arrived) in enumerate(((near_acc, near_in), (far_acc, far_in))):
        peaks = jnp.zeros((256, 128), jnp.float32)
        for label in range(5):
            partials[5 * part + label].wait_recv()
            numerator = acc[2 * label + core] + arrived[label]
            scores = numerator * numerator / divisor
            peaks = jnp.where(lanes == label, jnp.max(scores, axis=1, keepdims=True), peaks)
        peak_ref[:, 256 * part : 256 * part + 128] = jnp.transpose(peaks[0:128])[0:8, :]
        peak_ref[:, 256 * part + 128 : 256 * part + 256] = jnp.transpose(peaks[128:256])[0:8, :]
    found = jnp.where(mask_ref[0:1, :] > 0.0, peak_ref[...], 0.0)
    msg_ref[...] = jnp.zeros_like(msg_ref)
    for s in range(8):
        msg_ref[s, :, 0:64] = found[:, 64 * s : 64 * s + 64]

    sends = []
    for c in range(2):
        for s, o in enumerate(CORE_SLOTS[c]):
            for k in range(2):
                if o == 0 and k == c:
                    continue
                copy = remote(
                    msg_ref.at[s], msg_in.at[2 * SLOTS.index(o) + c], m_send.at[2 * s + k],
                    m_recv.at[2 * SLOTS.index(o) + c], (me + o, k),
                )
                condition = (core == c) if o == 0 else (core == c) & inside(o)
                when(condition, copy.start)
                sends.append((condition, copy))

    best = jnp.where(core == 0, msg_ref[2], msg_ref[1])
    for c in range(2):
        for o in CORE_SLOTS[c]:
            index = 2 * SLOTS.index(o) + c
            condition = (core == 1 - c) if o == 0 else inside(-o)
            copy = remote(msg_ref.at[0], msg_in.at[index], m_send.at[0], m_recv.at[index], sib)
            when(condition, copy.wait_recv)
            best = jnp.maximum(best, jnp.where(condition, msg_in[index], 0.0))
    pow_copy.wait_recv()
    power = pow_ref[...] + pow_other[...]
    result = jnp.sqrt(best / (power / (2.0 * half) + 1e-05))
    out_ref[...] = result[0:5, 0:64]

    for copy in g_copies + [env_copy, mom_copy, pow_copy] + partials:
        copy.wait_send()
    for o, copy in y_copies:
        when(inside(-o), copy.wait_send)
    for condition, copy in sends:
        when(condition, copy.wait_send)


def shards(genotypes, phenotypes, environment, shuffles, window_start, window_end, chrom_bounds):
    snps, half = genotypes.shape
    genes = phenotypes.shape[0]
    labels = shuffles.shape[0] + 1
    genome_size = lax.axis_size("genome")
    me = lax.axis_index("genome")
    core = lax.axis_index("sample")
    vmem = pl.BlockSpec(memory_space=pltpu.VMEM)

    shuffles_other = lax.ppermute(shuffles, "sample", [(0, 1), (1, 0)])
    inverse = pl.pallas_call(
        inverse_kernel,
        name="invert",
        out_shape=jax.ShapeDtypeStruct(((labels - 1) * half // 128, 128), jnp.int32),
        in_specs=[vmem, vmem],
        out_specs=vmem,
    )(shuffles, shuffles_other)

    total_blocks = snps * genome_size // SNP_BLOCK
    lower_edge, upper_edge = window_bounds(window_start, window_end, chrom_bounds, total_blocks)
    padding = jnp.zeros((4 * genes,), jnp.int32)
    edges = jnp.stack([
        jnp.concatenate([padding, lower_edge, padding]),
        jnp.concatenate([padding, upper_edge, padding]),
    ])
    band = lax.dynamic_slice_in_dim(edges, me * genes, 9 * genes, 1).reshape(2, 9, genes)
    block = me * (snps // SNP_BLOCK) + core
    hits = ((band[0] <= block) & (block < band[1])).astype(jnp.float32)
    masks = [
        jnp.concatenate([hits[o + 4] for o in CORE_SLOTS[c]]).reshape(1, 8 * genes) for c in range(2)
    ]
    mask = jnp.broadcast_to(jnp.where(core == 0, masks[0], masks[1]), (8, 8 * genes))

    f32, bf16 = jnp.float32, jnp.bfloat16
    dma = pltpu.SemaphoreType.DMA
    return pl.pallas_call(
        scan_kernel,
        name="scan",
        out_shape=jax.ShapeDtypeStruct((labels, genes), jnp.float32),
        in_specs=[pl.BlockSpec(memory_space=pltpu.SMEM), vmem, vmem, vmem, vmem],
        out_specs=vmem,
        scratch_shapes=[
            pltpu.VMEM((2 * half, 4, 128), f32),
            pltpu.VMEM((4 * half, snps), bf16),
            pltpu.VMEM((9 * genes, half), bf16),
            pltpu.VMEM((snps, half), bf16),
            pltpu.VMEM((half // 128, 128), f32),
            pltpu.VMEM((snps, 128), f32),
            pltpu.VMEM((snps, 128), f32),
            pltpu.VMEM((snps, 128), f32),
            pltpu.VMEM((8, snps), f32),
            pltpu.VMEM((STEP, 4, 128), f32),
            pltpu.VMEM((STEP, 4, 128), f32),
            pltpu.VMEM((2 * labels, 256, 256), f32),
            pltpu.VMEM((2 * labels, 256, 256), f32),
            pltpu.VMEM((labels, 256, 256), f32),
            pltpu.VMEM((labels, 256, 256), f32),
            pltpu.VMEM((8, 8 * genes), f32),
            pltpu.VMEM((8, 8, 128), f32),
            pltpu.VMEM((18, 8, 128), f32),
            pltpu.VMEM((8, 128), f32),
            pltpu.VMEM((8, 128), f32),
            dma((8,)), dma((8,)), dma((4,)), dma((4,)), dma((3,)), dma((3,)),
            dma((10,)), dma((10,)), dma((16,)), dma((18,)), dma(()),
        ],
        compiler_params=pltpu.CompilerParams(
            collective_id=0, has_side_effects=True, vmem_limit_bytes=64 * 1024 * 1024 - 65536
        ),
    )(inverse.reshape(-1), phenotypes, genotypes, environment.reshape(-1, 128), mask)


def solution(mesh):
    placed = (
        P("genome", "sample"),
        P("genome", "sample"),
        P("sample"),
        P(None, "sample"),
        P(),
        P(),
        P(),
    )
    return jax.shard_map(
        shards, mesh=mesh, in_specs=placed, out_specs=P(None, "genome"), check_vma=False
    )
```

```python
import functools

import jax
import jax.numpy as jnp
from jax import lax
from jax.experimental import pallas as pl
from jax.experimental.pallas import tpu as pltpu
from jax.sharding import PartitionSpec as P

SNP_BLOCK = 256
MESH = pl.DeviceIdType.MESH
SLOTS = (
    (-4, 3, 0, 1, 4, 2, -3, -2, -1),
    (-4, -1, 0, 1, 4, 2, -3, 3, -2),
    (-4, -1, 0, 1, 4, -2, -3, 3, 2),
    (-4, -1, 0, -3, 4, -2, 3, 2, 1),
)
CORE_SLOTS = ((0, 1, 2, 3, 5, 6, 7, 8), (1, 2, 3, 4, 5, 6, 7, 8))
STEP = 512
FAR_STEP = 1024
SPLIT = 2


def when(condition, action):
    if condition is None:
        action()
    else:
        pl.when(condition)(action)


def inverse_kernel(own_ref, other_ref, out_ref):
    core = lax.axis_index("sample")
    perms, half = own_ref.shape
    width = 2048
    rows = half // 128
    for p in range(perms):
        total = jnp.zeros((2 * rows, 128), jnp.float32)
        for part, ref in enumerate((own_ref, other_ref)):
            for start in range(0, half, width):
                target = ref[p : p + 1, start : start + width]
                high = (target >> 7) - rows * core
                low = target & 127
                place = lax.broadcasted_iota(jnp.int32, (1, width), 1) + (part * half + start)
                hit = lax.broadcasted_iota(jnp.int32, (rows, width), 0) == high
                place_high = (place >> 7).astype(jnp.float32)
                place_low = (place & 127).astype(jnp.float32)
                left = jnp.concatenate(
                    [jnp.where(hit, place_high, 0.0), jnp.where(hit, place_low, 0.0)], axis=0
                ).astype(jnp.bfloat16)
                right = jnp.where(
                    lax.broadcasted_iota(jnp.int32, (128, width), 0) == low, 1.0, 0.0
                ).astype(jnp.bfloat16)
                total += lax.dot_general(
                    left, right, (((1,), (1,)), ((), ())), preferred_element_type=jnp.float32
                )
        out_ref[p * rows : (p + 1) * rows, :] = (
            total[:rows] * 128.0 + total[rows:]
        ).astype(jnp.int32) * 4


def scan_kernel(
    inv_ref, bounds_ref, y_ref, g_ref, env_ref, start_ref, end_ref, out_ref,
    h_ref, gp_ref, band_ref, other_ref, env_other, mom_ref, mom_other, reg_ref, div_ref,
    stage0, stage1, near_acc, far_acc, near_in, far_in, peak_ref, msg_ref, msg_in, pow_ref, pow_other,
    y_send, y_recv, g_send, g_recv, s_send, s_recv, p_send, p_recv, m_send, m_recv, local_sem,
):
    me = lax.axis_index("genome")
    core = lax.axis_index("sample")
    indices = lax.axis_size("genome")
    sib = (me, 1 - core)
    genes, half = y_ref.shape
    snps = g_ref.shape[0]

    def inside(o):
        return (me + o >= 0) & (me + o < indices)

    barrier = pltpu.get_barrier_semaphore()
    pl.semaphore_signal(barrier, inc=1, device_id=sib, device_id_type=MESH)
    count = jnp.int32(1)
    for o in range(-4, 5):
        if o != 0:
            for k in range(2):
                @pl.when(inside(o))
                def _(o=o, k=k):
                    pl.semaphore_signal(barrier, inc=1, device_id=(me + o, k), device_id_type=MESH)
            count = count + jnp.where(inside(o), 2, 0)
    pl.semaphore_wait(barrier, count)

    def remote(src, dst, send, recv, target):
        return pltpu.make_async_remote_copy(
            src, dst, send, recv, device_id=target, device_id_type=MESH
        )

    width = half // 4
    g_copies = [
        remote(
            g_ref.at[:, pl.ds(i * width, width)], other_ref.at[:, pl.ds(i * width, width)],
            g_send.at[i], g_recv.at[i], sib,
        )
        for i in range(4)
    ]
    env_copy = remote(env_ref, env_other, s_send.at[0], s_recv.at[0], sib)
    place = lax.rem(me, 4)
    line = lax.div(me, 4)
    piece = genes // 2
    above, below = line > 0, line < indices // 4 - 1
    hops = []

    def slot_valid(slot):
        checks = []
        for x in range(4):
            o = SLOTS[x][slot]
            if not 0 <= x + o < 4:
                checks.append((place == x, above if x + o < 0 else below))
        return checks

    def slot_wait(slot, part):
        copy = remote(
            y_ref.at[pl.ds(0, piece), :], band_ref.at[pl.ds(slot * genes + part * piece, piece), :],
            y_send.at[0], y_recv.at[2 * slot + part], sib,
        )
        bad = None
        for at, exists in slot_valid(slot):
            term = at & jnp.logical_not(exists)
            bad = term if bad is None else bad | term
        when(None if bad is None else jnp.logical_not(bad), copy.wait_recv)

    def hop(x, link, shift, part):
        step = {"right": 1, "left": -1, "up": -4, "down": 4}[link]
        needs = set()
        if link in ("right", "left"):
            other = (x + step) % 4
            step = other - x
        else:
            other = x
            needs.add(link)
        if not 0 <= x + shift < 4:
            needs.add("up" if x + shift < 0 else "down")
        here = SLOTS[x].index(shift)
        there = SLOTS[other].index(shift - step)
        index = sum(1 for at, _ in hops if at == x)
        if shift == 0:
            source = y_ref.at[pl.ds(part * piece, piece), :]
        else:
            source = band_ref.at[pl.ds(here * genes + part * piece, piece), :]
        copy = remote(
            source, band_ref.at[pl.ds(there * genes + part * piece, piece), :],
            y_send.at[index], y_recv.at[2 * there + part], (me + step, core),
        )
        when(rows_exist(needs), copy.start)
        hops.append((x, needs))

    def rows_exist(needs):
        if needs == {"up", "down"}:
            return above & below
        return {"up": above, "down": below}[min(needs)] if needs else None

    def finish_hops():
        for x in range(4):
            @pl.when(place == x)
            def _(x=x):
                for index, needs in enumerate([needs for at, needs in hops if at == x]):
                    copy = remote(
                        y_ref.at[pl.ds(0, piece), :], band_ref.at[pl.ds(0, piece), :],
                        y_send.at[index], y_recv.at[0], sib,
                    )
                    when(rows_exist(needs), copy.wait_send)

    def first_hops():
        for x in range(4):
            @pl.when(place == x)
            def _(x=x):
                for part in range(2):
                    for link in ("right", "left", "down", "up"):
                        hop(x, link, 0, part)

    def second_hops():
        for slot in (1, 3, 0, 4):
            for part in range(2):
                slot_wait(slot, part)
        for x in range(4):
            @pl.when(place == x)
            def _(x=x):
                left, right = SLOTS[x][1], SLOTS[x][3]
                hop(x, "right", left, 1)
                hop(x, "left", right, 0)
                if x < 3:
                    for part in ((0, 1) if x == 0 else (1, 0)):
                        hop(x, "down", right, part)
                if x > 0:
                    for part in ((1, 0) if x == 3 else (0, 1)):
                        hop(x, "up", left, part)
                if x == 3:
                    hop(x, "right", -4, 0)
                    hop(x, "right", -4, 1)
                if x == 0:
                    hop(x, "left", 4, 0)
                    hop(x, "left", 4, 1)

    def third_hops():
        for part in range(2):
            slot_wait(5, part)
        for x in range(4):
            @pl.when(place == x)
            def _(x=x):
                if x == 0:
                    hop(x, "down", 2, 0)
                if x == 1:
                    hop(x, "down", 2, 0)
                if x == 2:
                    hop(x, "up", -2, 1)
                if x == 3:
                    hop(x, "up", -2, 1)
        middle = (place == 1) | (place == 2)
        for slot, part, exists in ((6, 1, above), (7, 0, below)):
            copy = remote(
                y_ref.at[pl.ds(0, piece), :], band_ref.at[pl.ds(slot * genes + part * piece, piece), :],
                y_send.at[0], y_recv.at[2 * slot + part], sib,
            )
            pl.when(middle & exists)(copy.wait_recv)
        for x in (1, 2):
            @pl.when(place == x)
            def _(x=x):
                hop(x, "left", -3, 1)
                hop(x, "right", 3, 0)

    def last_arrivals():
        for slot in (6, 7, 8):
            for part in range(2):
                early = {(6, 1): True, (7, 0): True}.get((slot, part), False)
                copy = remote(
                    y_ref.at[pl.ds(0, piece), :], band_ref.at[pl.ds(slot * genes + part * piece, piece), :],
                    y_send.at[0], y_recv.at[2 * slot + part], sib,
                )
                for x in range(4):
                    if early and x in (1, 2):
                        continue
                    o = SLOTS[x][slot]
                    exists = above if x + o < 0 else below
                    pl.when((place == x) & exists)(copy.wait_recv)

    own_copy = pltpu.make_async_copy(y_ref, band_ref.at[pl.ds(2 * genes, genes), :], local_sem)
    own_copy.start()
    env_copy.start()
    for copy in g_copies:
        copy.start()
    first_hops()

    lane = lax.broadcasted_iota(jnp.int32, (64, 128), 1)

    def moments(block, _):
        first = pl.multiple_of(block * 64, 64)
        square = jnp.zeros((64, 128), jnp.float32)
        cross = square
        inter = square
        for column in range(half // 128):
            value = g_ref[pl.ds(first, 64), column * 128 : (column + 1) * 128].astype(jnp.float32)
            weight = env_ref[column : column + 1, :]
            value = value * value
            once = value * weight
            square += value
            cross += once
            inter += once * weight
        square = jnp.sum(square, axis=1, keepdims=True)
        cross = jnp.sum(cross, axis=1, keepdims=True)
        inter = jnp.sum(inter, axis=1, keepdims=True)
        mom_ref[pl.ds(first, 64), :] = jnp.where(lane == 0, square, jnp.where(lane == 1, cross, inter))
        return 0

    lax.fori_loop(0, snps // 64, moments, 0)
    mom_copy = remote(mom_ref, mom_other, s_send.at[1], s_recv.at[1], sib)
    mom_copy.start()

    power = jnp.zeros((genes, 128), jnp.float32)
    for column in range(half // 128):
        value = y_ref[:, column * 128 : (column + 1) * 128].astype(jnp.float32)
        power += value * value
    power = jnp.broadcast_to(jnp.sum(power, axis=1, keepdims=True), (genes, 128))
    power = jnp.concatenate([power, power], axis=0)
    pow_ref[...] = jnp.transpose(power)[0:8, :]
    pow_copy = remote(pow_ref, pow_other, s_send.at[2], s_recv.at[2], sib)
    pow_copy.start()

    near_acc[...] = jnp.zeros_like(near_acc)
    far_acc[...] = jnp.zeros_like(far_acc)
    mom_copy.wait_recv()
    env_copy.wait_recv()
    for q in range(4):
        rows = slice(q * 128, (q + 1) * 128)
        total = mom_ref[rows, :] + mom_other[rows, :]
        square, cross, inter = total[:, 0:1], total[:, 1:2], total[:, 2:3]
        regression = cross / square
        divisor = inter - cross * regression + 0.1 * inter
        reg_ref[rows, :] = jnp.broadcast_to(regression, (128, 128))
        div_ref[:, rows] = jnp.transpose(jnp.broadcast_to(divisor, (128, 128)))[0:8, :]

    def residuals(source, weights, first, chunk):
        for s in range(2):
            start = pl.multiple_of(chunk * 256 + s * 128, 128)
            weight = weights[pl.ds(chunk * 2 + s, 1), :]
            for q in range(4):
                rows = slice(q * 128, (q + 1) * 128)
                value = source[rows, pl.ds(start, 128)].astype(jnp.float32)
                value = jnp.transpose(value * (weight - reg_ref[rows, :]))
                h_ref[pl.ds((first + start) * 4 + q, 128, stride=4), :] = value

    def own_residuals(chunk, _):
        residuals(g_ref, env_ref, 0, chunk)
        return 0

    lax.fori_loop(0, half // 256, own_residuals, 0)
    own_copy.wait()
    second_hops()

    def right_side(ref, first, b, count):
        return jnp.concatenate(
            [ref[pl.ds(first + 2 * b + i, count, stride=4), :] for i in range(2)], axis=1
        ).astype(jnp.bfloat16)

    def near_product(label, k, sides):
        for b in range(2):
            left = band_ref[64 * b : 64 * b + 256, pl.ds(pl.multiple_of(k * STEP, STEP), STEP)]
            near_acc[2 * label + b] += jnp.dot(left, sides[b], preferred_element_type=jnp.float32)

    def plain(k, _):
        near_product(0, k, [right_side(h_ref, k * (4 * STEP), b, STEP) for b in range(2)])
        return 0

    lax.fori_loop(0, half // STEP, plain, 0)

    for i in range(4):
        g_copies[i].wait_recv()

        def other_residuals(chunk, _):
            residuals(other_ref, env_other, half, chunk)
            return 0

        lax.fori_loop(i * width // 256, (i + 1) * width // 256, other_residuals, 0)

    per_label = half // STEP
    steps = 4 * per_label

    def gather(stage, n):
        base = n * STEP
        for t in range(STEP):
            stage[4 * t : 4 * t + 4, :] = h_ref[pl.ds(inv_ref[base + t], 4), :]

    def consume(stage, n):
        sides = [right_side(stage, 0, b, STEP) for b in range(2)]
        for b in range(2):
            gp_ref[pl.ds(pl.multiple_of(n * STEP, STEP), STEP), 256 * b : 256 * b + 256] = sides[b]
        near_product(1 + lax.div(n, per_label), lax.rem(n, per_label), sides)

    def permuted(i, _):
        n = 2 * i
        gather(stage1, n + 1)
        consume(stage0, n)
        gather(stage0, lax.rem(n + 2, steps))
        consume(stage1, n + 1)
        return 0

    gather(stage0, 0)
    lax.fori_loop(0, SPLIT, permuted, 0)
    third_hops()
    lax.fori_loop(SPLIT, steps // 2, permuted, 0)

    partials = []
    for label in range(5):
        copy = remote(
            near_acc.at[2 * label + 1 - core], near_in.at[label], p_send.at[label], p_recv.at[label], sib
        )
        copy.start()
        partials.append(copy)
    last_arrivals()

    for label in range(5):
        def distant(k, _, label=label):
            start = pl.multiple_of(k * FAR_STEP, FAR_STEP)
            left = band_ref[320:576, pl.ds(start, FAR_STEP)]
            for b in range(2):
                if label == 0:
                    side = right_side(h_ref, k * (4 * FAR_STEP), b, FAR_STEP)
                else:
                    side = gp_ref[pl.ds(start + (label - 1) * half, FAR_STEP), 256 * b : 256 * b + 256]
                far_acc[2 * label + b] += jnp.dot(left, side, preferred_element_type=jnp.float32)
            return 0

        lax.fori_loop(0, half // FAR_STEP, distant, 0)
        copy = remote(
            far_acc.at[2 * label + 1 - core], far_in.at[label], p_send.at[5 + label], p_recv.at[5 + label], sib
        )
        copy.start()
        partials.append(copy)

    divisor = div_ref[0:1, pl.ds(pl.multiple_of(core * 256, 256), 256)]
    lanes = lax.broadcasted_iota(jnp.int32, (256, 128), 1)
    for part, (acc, arrived) in enumerate(((near_acc, near_in), (far_acc, far_in))):
        peaks = jnp.zeros((256, 128), jnp.float32)
        for label in range(5):
            partials[5 * part + label].wait_recv()
            numerator = acc[2 * label + core] + arrived[label]
            scores = numerator * numerator / divisor
            peaks = jnp.where(lanes == label, jnp.max(scores, axis=1, keepdims=True), peaks)
        peak_ref[:, 256 * part : 256 * part + 128] = jnp.transpose(peaks[0:128])[0:8, :]
        peak_ref[:, 256 * part + 128 : 256 * part + 256] = jnp.transpose(peaks[128:256])[0:8, :]
    msg_ref[...] = jnp.zeros_like(msg_ref)
    shifts = [sum(jnp.where(place == x, SLOTS[x][slot], 0) for x in range(4)) for slot in range(9)]
    block = me * (snps // SNP_BLOCK) + core
    total_blocks = indices * (snps // SNP_BLOCK)
    for s in range(8):
        shift = jnp.where(core == 0, shifts[CORE_SLOTS[0][s]], shifts[CORE_SLOTS[1][s]])
        owner = jnp.clip(me + shift, 0, indices - 1)
        odd = lax.rem(owner, 2) == 1
        begin = start_ref[pl.ds(lax.div(owner, 2), 1), :]
        finish = end_ref[pl.ds(lax.div(owner, 2), 1), :]
        begin = jnp.where(odd, begin[:, 64:128], begin[:, 0:64])
        finish = jnp.where(odd, finish[:, 64:128], finish[:, 0:64])
        middle = (begin + finish - 1) >> 1
        lower = jnp.zeros_like(middle)
        upper = jnp.full_like(middle, total_blocks)
        for k in range(bounds_ref.shape[0]):
            bound = bounds_ref[k]
            before = bound <= middle
            lower = jnp.maximum(lower, jnp.where(before, bound, 0))
            upper = jnp.minimum(upper, jnp.where(before, total_blocks, bound))
        inner = (jnp.maximum(begin, lower) <= block) & (block < jnp.minimum(finish, upper))
        msg_ref[s, :, 0:64] = jnp.where(inner, peak_ref[:, 64 * s : 64 * s + 64], 0.0)

    sends = []
    for c in range(2):
        for s in range(8):
            for k in range(2):
                local = CORE_SLOTS[c][s] == 2
                if local and k == c:
                    continue
                shift = shifts[CORE_SLOTS[c][s]]
                copy = remote(
                    msg_ref.at[s], msg_in.at[2 * (shift + 4) + c], m_send.at[2 * s + k],
                    m_recv.at[2 * (shift + 4) + c], (me + shift, k),
                )
                condition = (core == c) & inside(shift)
                when(condition, copy.start)
                sends.append((condition, copy))

    best = jnp.where(core == 0, msg_ref[2], msg_ref[1])
    for c in range(2):
        for o in range(-4 + c, 4 + c):
            index = 2 * (o + 4) + c
            condition = (core == 1 - c) if o == 0 else inside(-o)
            copy = remote(msg_ref.at[0], msg_in.at[index], m_send.at[0], m_recv.at[index], sib)
            when(condition, copy.wait_recv)
            best = jnp.maximum(best, jnp.where(condition, msg_in[index], 0.0))
    pow_copy.wait_recv()
    power = pow_ref[...] + pow_other[...]
    result = jnp.sqrt(best / (power / (2.0 * half) + 1e-05))
    out_ref[...] = result[0:5, 0:64]

    for copy in g_copies + [env_copy, mom_copy, pow_copy] + partials:
        copy.wait_send()
    finish_hops()
    for condition, copy in sends:
        when(condition, copy.wait_send)


def shards(genotypes, phenotypes, environment, shuffles, window_start, window_end, chrom_bounds):
    snps, half = genotypes.shape
    genes = phenotypes.shape[0]
    labels = shuffles.shape[0] + 1
    vmem = pl.BlockSpec(memory_space=pltpu.VMEM)

    shuffles_other = lax.ppermute(shuffles, "sample", [(0, 1), (1, 0)])
    inverse = pl.pallas_call(
        inverse_kernel,
        name="invert",
        out_shape=jax.ShapeDtypeStruct(((labels - 1) * half // 128, 128), jnp.int32),
        in_specs=[vmem, vmem],
        out_specs=vmem,
    )(shuffles, shuffles_other)

    f32, bf16 = jnp.float32, jnp.bfloat16
    dma = pltpu.SemaphoreType.DMA
    return pl.pallas_call(
        scan_kernel,
        name="scan",
        out_shape=jax.ShapeDtypeStruct((labels, genes), jnp.float32),
        in_specs=[pl.BlockSpec(memory_space=pltpu.SMEM)] * 2 + [vmem] * 5,
        out_specs=vmem,
        scratch_shapes=[
            pltpu.VMEM((2 * half * 4, 128), f32),
            pltpu.VMEM((4 * half, snps), bf16),
            pltpu.VMEM((9 * genes, half), bf16),
            pltpu.VMEM((snps, half), bf16),
            pltpu.VMEM((half // 128, 128), f32),
            pltpu.VMEM((snps, 128), f32),
            pltpu.VMEM((snps, 128), f32),
            pltpu.VMEM((snps, 128), f32),
            pltpu.VMEM((8, snps), f32),
            pltpu.VMEM((4 * STEP, 128), f32),
            pltpu.VMEM((4 * STEP, 128), f32),
            pltpu.VMEM((2 * labels, 256, 256), f32),
            pltpu.VMEM((2 * labels, 256, 256), f32),
            pltpu.VMEM((labels, 256, 256), f32),
            pltpu.VMEM((labels, 256, 256), f32),
            pltpu.VMEM((8, 8 * genes), f32),
            pltpu.VMEM((8, 8, 128), f32),
            pltpu.VMEM((18, 8, 128), f32),
            pltpu.VMEM((8, 128), f32),
            pltpu.VMEM((8, 128), f32),
            dma((20,)), dma((18,)), dma((4,)), dma((4,)), dma((3,)), dma((3,)),
            dma((10,)), dma((10,)), dma((16,)), dma((18,)), dma(()),
        ],
        compiler_params=pltpu.CompilerParams(
            collective_id=0, has_side_effects=True, vmem_limit_bytes=64 * 1024 * 1024 - 65536
        ),
    )(
        inverse.reshape(-1), chrom_bounds, phenotypes, genotypes, environment.reshape(-1, 128),
        window_start.reshape(-1, 128), window_end.reshape(-1, 128),
    )


def solution(mesh):
    placed = (
        P("genome", "sample"),
        P("genome", "sample"),
        P("sample"),
        P(None, "sample"),
        P(),
        P(),
        P(),
    )
    return jax.shard_map(
        shards, mesh=mesh, in_specs=placed, out_specs=P(None, "genome"), check_vma=False
    )
```

```python
import functools

import jax
import jax.numpy as jnp
from jax import lax
from jax.experimental import pallas as pl
from jax.experimental.pallas import tpu as pltpu
from jax.sharding import PartitionSpec as P

SNP_BLOCK = 256
MESH = pl.DeviceIdType.MESH
SLOTS = (
    (-4, 3, 0, 1, 4, 2, -3, -2, -1),
    (-4, -1, 0, 1, 4, 2, -3, 3, -2),
    (-4, -1, 0, 1, 4, -2, -3, 3, 2),
    (-4, -1, 0, -3, 4, -2, 3, 2, 1),
)
CORE_SLOTS = ((0, 1, 2, 3, 5, 6, 7, 8), (1, 2, 3, 4, 5, 6, 7, 8))
STEP = 512
FAR_STEP = 1024


def when(condition, action):
    if condition is None:
        action()
    else:
        pl.when(condition)(action)


def remote(src, dst, send, recv, target):
    return pltpu.make_async_remote_copy(
        src, dst, send, recv, device_id=target, device_id_type=MESH
    )


def row_places(me, indices):
    place = lax.rem(me, 4)
    line = lax.div(me, 4)
    left = me - place + lax.rem(place + 3, 4)
    right = me - place + lax.rem(place + 1, 4)
    return place, left, right, line > 0, line < indices // 4 - 1


def residuals(source, weights, reg_ref, h_ref, k, first):
    for s in range(2):
        start = pl.multiple_of(k * 256 + s * 128, 128)
        weight = weights[pl.ds(k * 2 + s, 1), :]
        for q in range(4):
            rows = slice(q * 128, (q + 1) * 128)
            value = source[rows, pl.ds(start, 128)].astype(jnp.float32)
            value = jnp.transpose(value * (weight - reg_ref[rows, :]))
            h_ref[pl.ds((first + start) * 4 + q, 128, stride=4), :] = value


def exchange_kernel(
    shuffles_ref, env_ref, y_hbm, g_hbm,
    inv_ref, near_hbm, other_hbm, own_hbm, env_out, reg_ref, div_ref, pow_out,
    shuffles_other, env_other, y_ref, g_ref, h_ref, mom_ref, mom_other, pow_ref, pow_other,
    local_sem, h_sem, y_send, y_recv, g_send, g_recv, s_send, s_recv,
):
    me = lax.axis_index("genome")
    core = lax.axis_index("sample")
    indices = lax.axis_size("genome")
    sib = (me, 1 - core)
    perms, half = shuffles_ref.shape
    snps = g_hbm.shape[0]
    genes = y_hbm.shape[0]
    place, left, right, above, below = row_places(me, indices)
    part = snps // 4
    g_loads = [
        pltpu.make_async_copy(
            g_hbm.at[pl.ds(i * part, part), :], g_ref.at[pl.ds(i * part, part), :], local_sem.at[i]
        )
        for i in range(4)
    ]
    y_load = pltpu.make_async_copy(y_hbm, y_ref, local_sem.at[4])
    y_load.start()
    for copy in g_loads:
        copy.start()

    barrier = pltpu.get_barrier_semaphore()
    for target in (sib, (left, core), (right, core)):
        pl.semaphore_signal(barrier, inc=1, device_id=target, device_id_type=MESH)
    pl.when(above)(
        lambda: pl.semaphore_signal(barrier, inc=1, device_id=(me - 4, core), device_id_type=MESH)
    )
    pl.when(below)(
        lambda: pl.semaphore_signal(barrier, inc=1, device_id=(me + 4, core), device_id_type=MESH)
    )
    pl.semaphore_wait(barrier, 3 + jnp.where(above, 1, 0) + jnp.where(below, 1, 0))

    shuffle_copy = remote(shuffles_ref, shuffles_other, s_send.at[0], s_recv.at[0], sib)
    env_copy = remote(env_ref, env_other, s_send.at[1], s_recv.at[1], sib)
    shuffle_copy.start()
    env_copy.start()
    piece = genes // 2
    y_copies = []
    for h in range(2):
        for slot, target, sent, got in (
            (1, right, None, None), (2, left, None, None), (0, me + 4, below, above), (3, me - 4, above, below),
        ):
            copy = remote(
                y_hbm.at[pl.ds(h * piece, piece), :], near_hbm.at[pl.ds(slot * genes + h * piece, piece), :],
                y_send.at[2 * slot + h], y_recv.at[2 * slot + h], (target, core),
            )
            when(sent, copy.start)
            y_copies.append((sent, got, copy))
    g_copies = [
        remote(
            g_hbm.at[pl.ds(i * part, part), :], other_hbm.at[pl.ds(i * part, part), :],
            g_send.at[i], g_recv.at[i], sib,
        )
        for i in range(4)
    ]
    for copy in g_copies:
        copy.start()

    lane = lax.broadcasted_iota(jnp.int32, (64, 128), 1)

    def moments(block, _):
        first = pl.multiple_of(block * 64, 64)
        square = jnp.zeros((64, 128), jnp.float32)
        cross = square
        inter = square
        for column in range(half // 128):
            value = g_ref[pl.ds(first, 64), column * 128 : (column + 1) * 128].astype(jnp.float32)
            weight = env_ref[column : column + 1, :]
            value = value * value
            once = value * weight
            square += value
            cross += once
            inter += once * weight
        square = jnp.sum(square, axis=1, keepdims=True)
        cross = jnp.sum(cross, axis=1, keepdims=True)
        inter = jnp.sum(inter, axis=1, keepdims=True)
        mom_ref[pl.ds(first, 64), :] = jnp.where(lane == 0, square, jnp.where(lane == 1, cross, inter))
        return 0

    for copy in g_loads:
        copy.wait()
    lax.fori_loop(0, snps // 64, moments, 0)
    mom_copy = remote(mom_ref, mom_other, s_send.at[2], s_recv.at[2], sib)
    mom_copy.start()

    y_load.wait()
    power = jnp.zeros((genes, 128), jnp.float32)
    for column in range(half // 128):
        value = y_ref[:, column * 128 : (column + 1) * 128].astype(jnp.float32)
        power += value * value
    power = jnp.broadcast_to(jnp.sum(power, axis=1, keepdims=True), (genes, 128))
    power = jnp.concatenate([power, power], axis=0)
    pow_ref[...] = jnp.transpose(power)[0:8, :]
    pow_copy = remote(pow_ref, pow_other, s_send.at[3], s_recv.at[3], sib)
    pow_copy.start()

    width = 2048
    rows = half // 128

    def located(ref, p, offset):
        total = jnp.zeros((2 * rows, 128), jnp.float32)
        for start in range(0, half, width):
            target = ref[p : p + 1, start : start + width]
            high = (target >> 7) - rows * core
            low = target & 127
            spot = lax.broadcasted_iota(jnp.int32, (1, width), 1) + (offset + start)
            hit = lax.broadcasted_iota(jnp.int32, (rows, width), 0) == high
            spot_high = (spot >> 7).astype(jnp.float32)
            spot_low = (spot & 127).astype(jnp.float32)
            lhs = jnp.concatenate(
                [jnp.where(hit, spot_high, 0.0), jnp.where(hit, spot_low, 0.0)], axis=0
            ).astype(jnp.bfloat16)
            rhs = jnp.where(
                lax.broadcasted_iota(jnp.int32, (128, width), 0) == low, 1.0, 0.0
            ).astype(jnp.bfloat16)
            total += lax.dot_general(
                lhs, rhs, (((1,), (1,)), ((), ())), preferred_element_type=jnp.float32
            )
        return total

    totals = [located(shuffles_ref, p, 0) for p in range(perms)]
    mom_copy.wait_recv()
    for q in range(4):
        lines = slice(q * 128, (q + 1) * 128)
        total = mom_ref[lines, :] + mom_other[lines, :]
        square, cross, inter = total[:, 0:1], total[:, 1:2], total[:, 2:3]
        regression = cross / square
        divisor = inter - cross * regression + 0.1 * inter
        reg_ref[lines, :] = jnp.broadcast_to(regression, (128, 128))
        div_ref[:, lines] = jnp.transpose(jnp.broadcast_to(divisor, (128, 128)))[0:8, :]

    def own_residuals(k, _):
        residuals(g_ref, env_ref, reg_ref, h_ref, k, 0)
        return 0

    h_copies = []
    for i in range(4):
        lax.fori_loop(i * half // 1024, (i + 1) * half // 1024, own_residuals, 0)
        copy = pltpu.make_async_copy(
            h_ref.at[pl.ds(i * half, half), :], own_hbm.at[pl.ds(i * half, half), :], h_sem.at[i]
        )
        copy.start()
        h_copies.append(copy)

    shuffle_copy.wait_recv()
    for p in range(perms):
        total = totals[p] + located(shuffles_other, p, half)
        inv_ref[p * rows : (p + 1) * rows, :] = (
            total[:rows] * 128.0 + total[rows:]
        ).astype(jnp.int32) * 4

    env_copy.wait_recv()
    env_out[...] = env_other[...]
    pow_copy.wait_recv()
    pow_out[...] = pow_ref[...] + pow_other[...]
    for copy in h_copies:
        copy.wait()
    for copy in g_copies:
        copy.wait_recv()
    for sent, got, copy in y_copies:
        when(got, copy.wait_recv)
    for copy in g_copies + [shuffle_copy, env_copy, mom_copy, pow_copy]:
        copy.wait_send()
    for sent, got, copy in y_copies:
        when(sent, copy.wait_send)


def scan_kernel(
    inv_hbm, bounds_ref, y_hbm, other_hbm, own_hbm, near_hbm, env_other, reg_ref, div_ref, pow_ref, start_ref, end_ref,
    out_ref,
    index0, index1, h_ref, gp_ref, band_ref, other_ref,
    stage0, stage1, near_acc, far_acc, near_in, far_in, peak_ref, msg_ref, msg_in,
    y_send, y_recv, p_send, p_recv, m_send, m_recv, band_sem, g_sem, index_sem,
):
    me = lax.axis_index("genome")
    core = lax.axis_index("sample")
    indices = lax.axis_size("genome")
    sib = (me, 1 - core)
    genes, half = y_hbm.shape
    snps = other_hbm.shape[0]

    def inside(o):
        return (me + o >= 0) & (me + o < indices)

    barrier = pltpu.get_barrier_semaphore()
    pl.semaphore_signal(barrier, inc=1, device_id=sib, device_id_type=MESH)
    count = jnp.int32(1)
    for o in range(-4, 5):
        if o != 0:
            for k in range(2):
                @pl.when(inside(o))
                def _(o=o, k=k):
                    pl.semaphore_signal(barrier, inc=1, device_id=(me + o, k), device_id_type=MESH)
            count = count + jnp.where(inside(o), 2, 0)

    place, _, _, above, below = row_places(me, indices)
    piece = genes // 2
    hops = []

    def arrival(slot, part):
        return remote(
            y_hbm.at[pl.ds(0, piece), :], band_ref.at[pl.ds(slot * genes + part * piece, piece), :],
            y_send.at[0], y_recv.at[2 * (slot - 5) + part], sib,
        )

    def hop(x, link, shift, part):
        step = {"right": 1, "left": -1, "up": -4, "down": 4}[link]
        needs = set()
        if link in ("right", "left"):
            other = (x + step) % 4
            step = other - x
        else:
            other = x
            needs.add(link)
        if not 0 <= x + shift < 4:
            needs.add("up" if x + shift < 0 else "down")
        here = SLOTS[x].index(shift)
        there = SLOTS[other].index(shift - step)
        index = sum(1 for at, _ in hops if at == x)
        if here in (0, 1, 3, 4):
            source = near_hbm.at[pl.ds((0, 1, 0, 2, 3)[here] * genes + part * piece, piece), :]
        else:
            source = band_ref.at[pl.ds(here * genes + part * piece, piece), :]
        copy = remote(
            source, band_ref.at[pl.ds(there * genes + part * piece, piece), :],
            y_send.at[index], y_recv.at[2 * (there - 5) + part], (me + step, core),
        )
        when(rows_exist(needs), copy.start)
        hops.append((x, needs))

    def rows_exist(needs):
        if needs == {"up", "down"}:
            return above & below
        return {"up": above, "down": below}[min(needs)] if needs else None

    def finish_hops():
        for x in range(4):
            @pl.when(place == x)
            def _(x=x):
                for index, needs in enumerate([needs for at, needs in hops if at == x]):
                    copy = remote(
                        y_hbm.at[pl.ds(0, piece), :], band_ref.at[pl.ds(0, piece), :],
                        y_send.at[index], y_recv.at[0], sib,
                    )
                    when(rows_exist(needs), copy.wait_send)

    def second_hops():
        for x in range(4):
            @pl.when(place == x)
            def _(x=x):
                left, right = SLOTS[x][1], SLOTS[x][3]
                hop(x, "right", left, 1)
                hop(x, "left", right, 0)
                if x < 3:
                    for part in ((0, 1) if x == 0 else (1, 0)):
                        hop(x, "down", right, part)
                if x > 0:
                    for part in ((1, 0) if x == 3 else (0, 1)):
                        hop(x, "up", left, part)
                if x == 3:
                    hop(x, "right", -4, 0)
                    hop(x, "right", -4, 1)
                if x == 0:
                    hop(x, "left", 4, 0)
                    hop(x, "left", 4, 1)

    def third_hops():
        for part in range(2):
            arrival(5, part).wait_recv()
        for x in range(4):
            @pl.when(place == x)
            def _(x=x):
                if x == 0:
                    hop(x, "down", 2, 0)
                if x == 1:
                    hop(x, "down", 2, 0)
                if x == 2:
                    hop(x, "up", -2, 1)
                if x == 3:
                    hop(x, "up", -2, 1)
        middle = (place == 1) | (place == 2)
        for slot, part, exists in ((6, 1, above), (7, 0, below)):
            pl.when(middle & exists)(arrival(slot, part).wait_recv)
        for x in (1, 2):
            @pl.when(place == x)
            def _(x=x):
                hop(x, "left", -3, 1)
                hop(x, "right", 3, 0)

    def last_arrivals():
        for slot in (6, 7, 8):
            for part in range(2):
                early = {(6, 1): True, (7, 0): True}.get((slot, part), False)
                copy = arrival(slot, part)
                for x in range(4):
                    if early and x in (1, 2):
                        continue
                    o = SLOTS[x][slot]
                    exists = above if x + o < 0 else below
                    pl.when((place == x) & exists)(copy.wait_recv)

    band_loads = [pltpu.make_async_copy(y_hbm, band_ref.at[pl.ds(2 * genes, genes), :], band_sem.at[0])]
    for i, slot in enumerate((0, 1, 3, 4)):
        band_loads.append(pltpu.make_async_copy(
            near_hbm.at[pl.ds(i * genes, genes), :], band_ref.at[pl.ds(slot * genes, genes), :],
            band_sem.at[1 + i],
        ))
    width = half // 8
    other_loads = [
        pltpu.make_async_copy(
            other_hbm.at[:, pl.ds(i * width, width)], other_ref.at[:, pl.ds(i * width, width)], g_sem.at[i]
        )
        for i in range(8)
    ]
    own_load = pltpu.make_async_copy(own_hbm, h_ref.at[pl.ds(0, 4 * half), :], band_sem.at[5])
    index_rows = 1024
    blocks = 4 * half // index_rows

    def index_load(ref, slot, k):
        return pltpu.make_async_copy(
            inv_hbm.at[pl.ds(pl.multiple_of(k * index_rows, index_rows), index_rows)], ref, index_sem.at[slot]
        )

    for copy in other_loads:
        copy.start()
    own_load.start()
    for copy in band_loads:
        copy.start()
    index_load(index0, 0, 0).start()
    index_load(index1, 1, 1).start()

    def other_residuals(k, _):
        residuals(other_ref, env_other, reg_ref, h_ref, k, half)
        return 0

    near_acc[...] = jnp.zeros_like(near_acc)
    far_acc[...] = jnp.zeros_like(far_acc)
    for i, copy in enumerate(other_loads):
        copy.wait()
        lax.fori_loop(i * width // 256, (i + 1) * width // 256, other_residuals, 0)
        if i == 1:
            pl.semaphore_wait(barrier, count)
            second_hops()
    own_load.wait()
    for copy in band_loads:
        copy.wait()

    def right_side(ref, first, b, count):
        return jnp.concatenate(
            [ref[pl.ds(first + 2 * b + i, count, stride=4), :] for i in range(2)], axis=1
        ).astype(jnp.bfloat16)

    def gather(stage, index, offset):
        for t in range(STEP):
            stage[4 * t : 4 * t + 4, :] = h_ref[pl.ds(index[offset + t], 4), :]

    def settle(stage, n):
        for q in range(4):
            gp_ref[pl.ds(pl.multiple_of((n + 1) * STEP, STEP), STEP), 128 * q : 128 * q + 128] = (
                stage[pl.ds(q, STEP, stride=4), :].astype(jnp.bfloat16)
            )

    def product(acc, rows, label, k, base, plain):
        start = pl.multiple_of(k * FAR_STEP, FAR_STEP)
        for b in range(2):
            lhs = band_ref[rows[b] : rows[b] + 256, pl.ds(start, FAR_STEP)]
            if plain:
                rhs = right_side(h_ref, start * 4, b, FAR_STEP)
            else:
                rhs = gp_ref[pl.ds(pl.multiple_of(base + start, STEP), FAR_STEP), 256 * b : 256 * b + 256]
            acc[2 * label + b] += jnp.dot(lhs, rhs, preferred_element_type=jnp.float32)

    near_rows, far_rows = (0, 64), (320, 320)

    def permuted(i, _, plain=False):
        for s, (index, slot) in enumerate(((index0, 0), (index1, 1))):
            index_load(index, slot, 2 * i + s).wait()
            n = 4 * i + 2 * s
            gather(stage0, index, 0)
            settle(stage1, n - 1)
            label = lax.div(i, 2)
            product(near_acc, near_rows, label, lax.rem(2 * i + s, 4), STEP + (label - 1) * half, plain)
            gather(stage1, index, STEP)
            settle(stage0, n)
            index_load(index, slot, lax.rem(2 * i + s + 2, blocks)).start()
        return 0

    lax.fori_loop(0, 2, functools.partial(permuted, plain=True), 0)
    third_hops()
    lax.fori_loop(2, blocks // 2, permuted, 0)
    settle(stage1, 4 * half // STEP - 1)
    index_load(index0, 0, 0).wait()
    index_load(index1, 1, 1).wait()

    def last_near(k, _):
        product(near_acc, near_rows, 4, k, STEP + 3 * half, False)
        return 0

    lax.fori_loop(0, half // FAR_STEP, last_near, 0)

    partials = []
    for label in range(5):
        copy = remote(
            near_acc.at[2 * label + 1 - core], near_in.at[label], p_send.at[label], p_recv.at[label], sib
        )
        copy.start()
        partials.append(copy)
    last_arrivals()

    for label in range(5):
        def distant(k, _, label=label):
            product(far_acc, far_rows, label, k, STEP + (label - 1) * half, label == 0)
            return 0

        lax.fori_loop(0, half // FAR_STEP, distant, 0)
        copy = remote(
            far_acc.at[2 * label + 1 - core], far_in.at[label], p_send.at[5 + label], p_recv.at[5 + label], sib
        )
        copy.start()
        partials.append(copy)

    divisor = div_ref[0:1, pl.ds(pl.multiple_of(core * 256, 256), 256)]
    lanes = lax.broadcasted_iota(jnp.int32, (256, 128), 1)
    for part, (acc, arrived) in enumerate(((near_acc, near_in), (far_acc, far_in))):
        peaks = jnp.zeros((256, 128), jnp.float32)
        for label in range(5):
            partials[5 * part + label].wait_recv()
            numerator = acc[2 * label + core] + arrived[label]
            scores = numerator * numerator / divisor
            peaks = jnp.where(lanes == label, jnp.max(scores, axis=1, keepdims=True), peaks)
        peak_ref[:, 256 * part : 256 * part + 128] = jnp.transpose(peaks[0:128])[0:8, :]
        peak_ref[:, 256 * part + 128 : 256 * part + 256] = jnp.transpose(peaks[128:256])[0:8, :]
    msg_ref[...] = jnp.zeros_like(msg_ref)
    shifts = [sum(jnp.where(place == x, SLOTS[x][slot], 0) for x in range(4)) for slot in range(9)]
    block = me * (snps // SNP_BLOCK) + core
    total_blocks = indices * (snps // SNP_BLOCK)
    for s in range(8):
        shift = jnp.where(core == 0, shifts[CORE_SLOTS[0][s]], shifts[CORE_SLOTS[1][s]])
        owner = jnp.clip(me + shift, 0, indices - 1)
        odd = lax.rem(owner, 2) == 1
        begin = start_ref[pl.ds(lax.div(owner, 2), 1), :]
        finish = end_ref[pl.ds(lax.div(owner, 2), 1), :]
        begin = jnp.where(odd, begin[:, 64:128], begin[:, 0:64])
        finish = jnp.where(odd, finish[:, 64:128], finish[:, 0:64])
        middle = (begin + finish - 1) >> 1
        lower = jnp.zeros_like(middle)
        upper = jnp.full_like(middle, total_blocks)
        for k in range(bounds_ref.shape[0]):
            bound = bounds_ref[k]
            before = bound <= middle
            lower = jnp.maximum(lower, jnp.where(before, bound, 0))
            upper = jnp.minimum(upper, jnp.where(before, total_blocks, bound))
        inner = (jnp.maximum(begin, lower) <= block) & (block < jnp.minimum(finish, upper))
        msg_ref[s, :, 0:64] = jnp.where(inner, peak_ref[:, 64 * s : 64 * s + 64], 0.0)

    sends = []
    for c in range(2):
        for s in range(8):
            for k in range(2):
                local = CORE_SLOTS[c][s] == 2
                if local and k == c:
                    continue
                shift = shifts[CORE_SLOTS[c][s]]
                copy = remote(
                    msg_ref.at[s], msg_in.at[2 * (shift + 4) + c], m_send.at[2 * s + k],
                    m_recv.at[2 * (shift + 4) + c], (me + shift, k),
                )
                condition = (core == c) & inside(shift)
                when(condition, copy.start)
                sends.append((condition, copy))

    best = jnp.where(core == 0, msg_ref[2], msg_ref[1])
    for c in range(2):
        for o in range(-4 + c, 4 + c):
            index = 2 * (o + 4) + c
            condition = (core == 1 - c) if o == 0 else inside(-o)
            copy = remote(msg_ref.at[0], msg_in.at[index], m_send.at[0], m_recv.at[index], sib)
            when(condition, copy.wait_recv)
            best = jnp.maximum(best, jnp.where(condition, msg_in[index], 0.0))
    result = jnp.sqrt(best / (pow_ref[...] / (2.0 * half) + 1e-05))
    out_ref[...] = result[0:5, 0:64]

    for copy in partials:
        copy.wait_send()
    finish_hops()
    for condition, copy in sends:
        when(condition, copy.wait_send)


def shards(genotypes, phenotypes, environment, shuffles, window_start, window_end, chrom_bounds):
    snps, half = genotypes.shape
    genes = phenotypes.shape[0]
    labels = shuffles.shape[0] + 1
    vmem = pl.BlockSpec(memory_space=pltpu.VMEM)

    f32, bf16, i32 = jnp.float32, jnp.bfloat16, jnp.int32
    dma = pltpu.SemaphoreType.DMA
    shape = jax.ShapeDtypeStruct
    anywhere = pl.BlockSpec(memory_space=pl.ANY)
    smem = pl.BlockSpec(memory_space=pltpu.SMEM)
    weights = environment.reshape(-1, 128)
    lines = half // 128
    inverse, near, other, own, weights_other, slopes, divisors, power = pl.pallas_call(
        exchange_kernel,
        name="exchange",
        out_shape=(
            shape(((labels - 1) * lines, 128), i32),
            shape((4 * genes, half), bf16),
            shape((snps, half), bf16),
            shape((4 * half, 128), f32),
            shape((lines, 128), f32),
            shape((snps, 128), f32),
            shape((8, snps), f32),
            shape((8, 128), f32),
        ),
        in_specs=[vmem, vmem, anywhere, anywhere],
        out_specs=(vmem, anywhere, anywhere, anywhere, vmem, vmem, vmem, vmem),
        scratch_shapes=[
            pltpu.VMEM((labels - 1, half), i32),
            pltpu.VMEM((lines, 128), f32),
            pltpu.VMEM((genes, half), bf16),
            pltpu.VMEM((snps, half), bf16),
            pltpu.VMEM((4 * half, 128), f32),
            pltpu.VMEM((snps, 128), f32),
            pltpu.VMEM((snps, 128), f32),
            pltpu.VMEM((8, 128), f32),
            pltpu.VMEM((8, 128), f32),
            dma((5,)), dma((4,)), dma((8,)), dma((8,)), dma((4,)), dma((4,)), dma((4,)), dma((4,)),
        ],
        compiler_params=pltpu.CompilerParams(
            collective_id=1, has_side_effects=True, vmem_limit_bytes=64 * 1024 * 1024 - 65536
        ),
    )(shuffles, weights, phenotypes, genotypes)

    return pl.pallas_call(
        scan_kernel,
        name="scan",
        out_shape=shape((labels, genes), f32),
        in_specs=[anywhere, smem] + [anywhere] * 4 + [vmem] * 6,
        out_specs=vmem,
        scratch_shapes=[
            pltpu.SMEM((1024,), i32),
            pltpu.SMEM((1024,), i32),
            pltpu.VMEM((2 * half * 4, 128), f32),
            pltpu.VMEM((4 * half + STEP, snps), bf16),
            pltpu.VMEM((9 * genes, half), bf16),
            pltpu.VMEM((snps, half), bf16),
            pltpu.VMEM((4 * STEP, 128), f32),
            pltpu.VMEM((4 * STEP, 128), f32),
            pltpu.VMEM((2 * labels, 256, 256), f32),
            pltpu.VMEM((2 * labels, 256, 256), f32),
            pltpu.VMEM((labels, 256, 256), f32),
            pltpu.VMEM((labels, 256, 256), f32),
            pltpu.VMEM((8, 8 * genes), f32),
            pltpu.VMEM((8, 8, 128), f32),
            pltpu.VMEM((18, 8, 128), f32),
            dma((16,)), dma((8,)), dma((10,)), dma((10,)), dma((16,)), dma((18,)),
            dma((6,)), dma((8,)), dma((2,)),
        ],
        compiler_params=pltpu.CompilerParams(
            collective_id=0, has_side_effects=True, vmem_limit_bytes=64 * 1024 * 1024 - 65536
        ),
    )(
        inverse.reshape(-1), chrom_bounds, phenotypes, other, own, near, weights_other, slopes, divisors,
        power, window_start.reshape(-1, 128), window_end.reshape(-1, 128),
    )


def solution(mesh):
    placed = (
        P("genome", "sample"),
        P("genome", "sample"),
        P("sample"),
        P(None, "sample"),
        P(),
        P(),
        P(),
    )
    return jax.shard_map(
        shards, mesh=mesh, in_specs=placed, out_specs=P(None, "genome"), check_vma=False
    )
```

```python
import functools

import jax
import jax.numpy as jnp
from jax import lax
from jax.experimental import pallas as pl
from jax.experimental.pallas import tpu as pltpu
from jax.sharding import PartitionSpec as P

SNP_BLOCK = 256
MESH = pl.DeviceIdType.MESH
SLOTS = (
    (-4, 3, 0, 1, 4, 2, -3, -2, -1),
    (-4, -1, 0, 1, 4, 2, -3, 3, -2),
    (-4, -1, 0, 1, 4, -2, -3, 3, 2),
    (-4, -1, 0, -3, 4, -2, 3, 2, 1),
)
CORE_SLOTS = ((0, 1, 2, 3, 5, 6, 7, 8), (1, 2, 3, 4, 5, 6, 7, 8))
STEP = 512
FAR_STEP = 1024
SPLIT = 3


def when(condition, action):
    if condition is None:
        action()
    else:
        pl.when(condition)(action)


def remote(src, dst, send, recv, target):
    return pltpu.make_async_remote_copy(
        src, dst, send, recv, device_id=target, device_id_type=MESH
    )


def residuals(source, weights, reg_ref, h_ref, k, first):
    for s in range(2):
        start = pl.multiple_of(k * 256 + s * 128, 128)
        weight = weights[pl.ds(k * 2 + s, 1), :]
        for q in range(4):
            rows = slice(q * 128, (q + 1) * 128)
            value = source[rows, pl.ds(start, 128)].astype(jnp.float32)
            value = jnp.transpose(value * (weight - reg_ref[rows, :]))
            h_ref[pl.ds((first + start) * 4 + q, 128, stride=4), :] = value


def scan_kernel(
    bounds_ref, shuffles_ref, env_ref, start_ref, end_ref, y_hbm, g_hbm,
    out_ref,
    index0, index1, h_ref, gp_ref, band_ref, g_ref, other_ref, shuffles_other, env_other, inv_ref,
    mom_ref, mom_other, reg_ref, div_ref, pow_ref, pow_other,
    stage0, stage1, near_acc, far_acc, near_in, far_in, peak_ref, msg_ref, msg_in,
    y_send, y_recv, g_send, g_recv, s_send, s_recv, p_send, p_recv, m_send, m_recv,
    local_sem, index_sem,
):
    me = lax.axis_index("genome")
    core = lax.axis_index("sample")
    indices = lax.axis_size("genome")
    sib = (me, 1 - core)
    perms, half = shuffles_ref.shape
    genes = y_hbm.shape[0]
    snps = g_hbm.shape[0]
    quarter = snps // 4
    g_loads = [
        pltpu.make_async_copy(
            g_hbm.at[pl.ds(i * quarter, quarter), :], g_ref.at[pl.ds(i * quarter, quarter), :], local_sem.at[i]
        )
        for i in range(4)
    ]
    y_load = pltpu.make_async_copy(y_hbm, band_ref.at[pl.ds(2 * genes, genes), :], local_sem.at[4])
    for copy in g_loads:
        copy.start()
    y_load.start()

    def inside(o):
        return (me + o >= 0) & (me + o < indices)

    barrier = pltpu.get_barrier_semaphore()
    pl.semaphore_signal(barrier, inc=1, device_id=sib, device_id_type=MESH)
    count = jnp.int32(1)
    for o in range(-4, 5):
        if o != 0:
            for k in range(2):
                @pl.when(inside(o))
                def _(o=o, k=k):
                    pl.semaphore_signal(barrier, inc=1, device_id=(me + o, k), device_id_type=MESH)
            count = count + jnp.where(inside(o), 2, 0)
    pl.semaphore_wait(barrier, count)

    place = lax.rem(me, 4)
    line = lax.div(me, 4)
    above, below = line > 0, line < indices // 4 - 1
    piece = genes // 2
    hops = []

    def arrival(slot, part):
        return remote(
            y_hbm.at[pl.ds(0, piece), :], band_ref.at[pl.ds(slot * genes + part * piece, piece), :],
            y_send.at[0], y_recv.at[2 * slot + part], sib,
        )

    def hop(x, link, shift, part):
        step = {"right": 1, "left": -1, "up": -4, "down": 4}[link]
        needs = set()
        if link in ("right", "left"):
            other = (x + step) % 4
            step = other - x
        else:
            other = x
            needs.add(link)
        if not 0 <= x + shift < 4:
            needs.add("up" if x + shift < 0 else "down")
        here = SLOTS[x].index(shift)
        there = SLOTS[other].index(shift - step)
        index = sum(1 for at, _ in hops if at == x)
        if shift == 0:
            source = y_hbm.at[pl.ds(part * piece, piece), :]
        else:
            source = band_ref.at[pl.ds(here * genes + part * piece, piece), :]
        copy = remote(
            source, band_ref.at[pl.ds(there * genes + part * piece, piece), :],
            y_send.at[index], y_recv.at[2 * there + part], (me + step, core),
        )
        when(rows_exist(needs), copy.start)
        hops.append((x, needs))

    def rows_exist(needs):
        if needs == {"up", "down"}:
            return above & below
        return {"up": above, "down": below}[min(needs)] if needs else None

    def finish_hops():
        for x in range(4):
            @pl.when(place == x)
            def _(x=x):
                for index, needs in enumerate([needs for at, needs in hops if at == x]):
                    copy = remote(
                        y_hbm.at[pl.ds(0, piece), :], band_ref.at[pl.ds(0, piece), :],
                        y_send.at[index], y_recv.at[0], sib,
                    )
                    when(rows_exist(needs), copy.wait_send)

    def at_place(x):
        return pl.when(place == x)

    def first_hops():
        for x in range(4):
            @at_place(x)
            def _(x=x):
                for part in range(2):
                    for link in ("right", "left", "down", "up"):
                        hop(x, link, 0, part)

    def second_hops(part):
        arrival(1, part).wait_recv()
        arrival(3, part).wait_recv()
        pl.when(above)(arrival(0, part).wait_recv)
        pl.when(below)(arrival(4, part).wait_recv)
        for x in range(4):
            @at_place(x)
            def _(x=x):
                left, right = SLOTS[x][1], SLOTS[x][3]
                if part == 0:
                    hop(x, "left", right, 0)
                else:
                    hop(x, "right", left, 1)
                if x < 3:
                    hop(x, "down", right, part)
                if x > 0:
                    hop(x, "up", left, part)
                if x == 3:
                    hop(x, "right", -4, part)
                if x == 0:
                    hop(x, "left", 4, part)

    def third_hops():
        for part in range(2):
            arrival(5, part).wait_recv()
        for x in range(4):
            @at_place(x)
            def _(x=x):
                if x < 2:
                    hop(x, "down", 2, 1)
                else:
                    hop(x, "up", -2, 1)
        inner = (place == 1) | (place == 2)
        pl.when(inner & above)(arrival(6, 0).wait_recv)
        pl.when(inner & below)(arrival(7, 0).wait_recv)
        for x in (1, 2):
            @at_place(x)
            def _(x=x):
                hop(x, "left", -3, 0)
                hop(x, "right", 3, 0)

    def last_arrivals():
        for slot in (6, 7, 8):
            for part in range(2):
                early = slot in (6, 7) and part == 0
                copy = arrival(slot, part)
                for x in range(4):
                    if early and x in (1, 2):
                        continue
                    o = SLOTS[x][slot]
                    exists = above if x + o < 0 else below
                    pl.when((place == x) & exists)(copy.wait_recv)

    shuffle_copy = remote(shuffles_ref, shuffles_other, s_send.at[0], s_recv.at[0], sib)
    env_copy = remote(env_ref, env_other, s_send.at[1], s_recv.at[1], sib)
    shuffle_copy.start()
    env_copy.start()
    first_hops()
    g_copies = [
        remote(
            g_hbm.at[pl.ds(i * quarter, quarter), :], other_ref.at[pl.ds(i * quarter, quarter), :],
            g_send.at[i], g_recv.at[i], sib,
        )
        for i in range(4)
    ]
    for copy in g_copies:
        copy.start()

    lane = lax.broadcasted_iota(jnp.int32, (64, 128), 1)

    def moments(block, _):
        first = pl.multiple_of(block * 64, 64)
        square = jnp.zeros((64, 128), jnp.float32)
        cross = square
        inter = square
        for column in range(half // 128):
            value = g_ref[pl.ds(first, 64), column * 128 : (column + 1) * 128].astype(jnp.float32)
            weight = env_ref[column : column + 1, :]
            value = value * value
            once = value * weight
            square += value
            cross += once
            inter += once * weight
        square = jnp.sum(square, axis=1, keepdims=True)
        cross = jnp.sum(cross, axis=1, keepdims=True)
        inter = jnp.sum(inter, axis=1, keepdims=True)
        mom_ref[pl.ds(first, 64), :] = jnp.where(lane == 0, square, jnp.where(lane == 1, cross, inter))
        return 0

    for copy in g_loads:
        copy.wait()
    lax.fori_loop(0, snps // 64, moments, 0)
    mom_copy = remote(mom_ref, mom_other, s_send.at[2], s_recv.at[2], sib)
    mom_copy.start()

    y_load.wait()
    power = jnp.zeros((genes, 128), jnp.float32)
    for column in range(half // 128):
        value = band_ref[2 * genes : 3 * genes, column * 128 : (column + 1) * 128].astype(jnp.float32)
        power += value * value
    power = jnp.broadcast_to(jnp.sum(power, axis=1, keepdims=True), (genes, 128))
    power = jnp.concatenate([power, power], axis=0)
    pow_ref[...] = jnp.transpose(power)[0:8, :]
    pow_copy = remote(pow_ref, pow_other, s_send.at[3], s_recv.at[3], sib)
    pow_copy.start()

    near_acc[...] = jnp.zeros_like(near_acc)
    far_acc[...] = jnp.zeros_like(far_acc)
    width = 2048
    rows = half // 128

    def located(ref, p, offset):
        total = jnp.zeros((2 * rows, 128), jnp.float32)
        for start in range(0, half, width):
            target = ref[p : p + 1, start : start + width]
            high = (target >> 7) - rows * core
            low = target & 127
            spot = lax.broadcasted_iota(jnp.int32, (1, width), 1) + (offset + start)
            hit = lax.broadcasted_iota(jnp.int32, (rows, width), 0) == high
            spot_high = (spot >> 7).astype(jnp.float32)
            spot_low = (spot & 127).astype(jnp.float32)
            lhs = jnp.concatenate(
                [jnp.where(hit, spot_high, 0.0), jnp.where(hit, spot_low, 0.0)], axis=0
            ).astype(jnp.bfloat16)
            rhs = jnp.where(
                lax.broadcasted_iota(jnp.int32, (128, width), 0) == low, 1.0, 0.0
            ).astype(jnp.bfloat16)
            total += lax.dot_general(
                lhs, rhs, (((1,), (1,)), ((), ())), preferred_element_type=jnp.float32
            )
        return total

    totals = [located(shuffles_ref, p, 0) for p in range(perms)]
    mom_copy.wait_recv()
    for q in range(4):
        lines = slice(q * 128, (q + 1) * 128)
        total = mom_ref[lines, :] + mom_other[lines, :]
        square, cross, inter = total[:, 0:1], total[:, 1:2], total[:, 2:3]
        regression = cross / square
        divisor = inter - cross * regression + 0.1 * inter
        reg_ref[lines, :] = jnp.broadcast_to(regression, (128, 128))
        div_ref[:, lines] = jnp.transpose(jnp.broadcast_to(divisor, (128, 128)))[0:8, :]

    def own_residuals(k, _):
        residuals(g_ref, env_ref, reg_ref, h_ref, k, 0)
        return 0

    lax.fori_loop(0, half // 256, own_residuals, 0)
    second_hops(0)
    shuffle_copy.wait_recv()
    for p in range(perms):
        total = totals[p] + located(shuffles_other, p, half)
        spot = (total[:rows] * 128.0 + total[rows:]).astype(jnp.int32)
        inv_ref[p * rows : (p + 1) * rows, :] = jnp.minimum(jnp.maximum(spot, 0), 2 * half - 1) * 4

    index_rows = 1024
    blocks = 4 * half // index_rows

    def index_load(ref, slot, k):
        return pltpu.make_async_copy(
            inv_ref.at[pl.ds(pl.multiple_of(k * 8, 8), 8), :], ref, index_sem.at[slot]
        )

    index_load(index0, 0, 0).start()
    index_load(index1, 1, 1).start()

    def other_residuals(k, _):
        residuals(other_ref, env_other, reg_ref, h_ref, k, half)
        return 0

    env_copy.wait_recv()
    for copy in g_copies:
        copy.wait_recv()
    lax.fori_loop(0, half // 256, other_residuals, 0)
    second_hops(1)

    def right_side(ref, first, b, count):
        return jnp.concatenate(
            [ref[pl.ds(first + 2 * b + i, count, stride=4), :] for i in range(2)], axis=1
        ).astype(jnp.bfloat16)

    def gather(stage, index, offset):
        for t in range(STEP):
            stage[4 * t : 4 * t + 4, :] = h_ref[pl.ds(index[(offset + t) // 128, (offset + t) % 128], 4), :]

    def settle(stage, n):
        for q in range(4):
            gp_ref[pl.ds(pl.multiple_of((n + 1) * STEP, STEP), STEP), 128 * q : 128 * q + 128] = (
                stage[pl.ds(q, STEP, stride=4), :].astype(jnp.bfloat16)
            )

    def product(acc, rows, label, k, base, plain):
        start = pl.multiple_of(k * FAR_STEP, FAR_STEP)
        for b in range(2):
            lhs = band_ref[rows[b] : rows[b] + 256, pl.ds(start, FAR_STEP)]
            if plain:
                rhs = right_side(h_ref, start * 4, b, FAR_STEP)
            else:
                rhs = gp_ref[pl.ds(pl.multiple_of(base + start, STEP), FAR_STEP), 256 * b : 256 * b + 256]
            acc[2 * label + b] += jnp.dot(lhs, rhs, preferred_element_type=jnp.float32)

    near_rows, far_rows = (0, 64), (320, 320)

    def permuted(i, _, plain=False):
        for s, (index, slot) in enumerate(((index0, 0), (index1, 1))):
            index_load(index, slot, 2 * i + s).wait()
            n = 4 * i + 2 * s
            gather(stage0, index, 0)
            settle(stage1, n - 1)
            label = lax.div(i, 2)
            product(near_acc, near_rows, label, lax.rem(2 * i + s, 4), STEP + (label - 1) * half, plain)
            gather(stage1, index, STEP)
            settle(stage0, n)
            index_load(index, slot, lax.rem(2 * i + s + 2, blocks)).start()
        return 0

    lax.fori_loop(0, 2, functools.partial(permuted, plain=True), 0)
    lax.fori_loop(2, SPLIT, permuted, 0)
    third_hops()
    lax.fori_loop(SPLIT, blocks // 2, permuted, 0)
    settle(stage1, 4 * half // STEP - 1)
    index_load(index0, 0, 0).wait()
    index_load(index1, 1, 1).wait()

    def last_near(k, _):
        product(near_acc, near_rows, 4, k, STEP + 3 * half, False)
        return 0

    lax.fori_loop(0, half // FAR_STEP, last_near, 0)

    partials = []
    for label in range(5):
        copy = remote(
            near_acc.at[2 * label + 1 - core], near_in.at[label], p_send.at[label], p_recv.at[label], sib
        )
        copy.start()
        partials.append(copy)
    last_arrivals()

    for label in range(5):
        def distant(k, _, label=label):
            product(far_acc, far_rows, label, k, STEP + (label - 1) * half, label == 0)
            return 0

        lax.fori_loop(0, half // FAR_STEP, distant, 0)
        copy = remote(
            far_acc.at[2 * label + 1 - core], far_in.at[label], p_send.at[5 + label], p_recv.at[5 + label], sib
        )
        copy.start()
        partials.append(copy)

    divisor = div_ref[0:1, pl.ds(pl.multiple_of(core * 256, 256), 256)]
    lanes = lax.broadcasted_iota(jnp.int32, (256, 128), 1)
    for part, (acc, arrived) in enumerate(((near_acc, near_in), (far_acc, far_in))):
        peaks = jnp.zeros((256, 128), jnp.float32)
        for label in range(5):
            partials[5 * part + label].wait_recv()
            numerator = acc[2 * label + core] + arrived[label]
            scores = numerator * numerator / divisor
            peaks = jnp.where(lanes == label, jnp.max(scores, axis=1, keepdims=True), peaks)
        peak_ref[:, 256 * part : 256 * part + 128] = jnp.transpose(peaks[0:128])[0:8, :]
        peak_ref[:, 256 * part + 128 : 256 * part + 256] = jnp.transpose(peaks[128:256])[0:8, :]
    msg_ref[...] = jnp.zeros_like(msg_ref)
    shifts = [sum(jnp.where(place == x, SLOTS[x][slot], 0) for x in range(4)) for slot in range(9)]
    block = me * (snps // SNP_BLOCK) + core
    total_blocks = indices * (snps // SNP_BLOCK)
    for s in range(8):
        shift = jnp.where(core == 0, shifts[CORE_SLOTS[0][s]], shifts[CORE_SLOTS[1][s]])
        owner = jnp.clip(me + shift, 0, indices - 1)
        odd = lax.rem(owner, 2) == 1
        begin = start_ref[pl.ds(lax.div(owner, 2), 1), :]
        finish = end_ref[pl.ds(lax.div(owner, 2), 1), :]
        begin = jnp.where(odd, begin[:, 64:128], begin[:, 0:64])
        finish = jnp.where(odd, finish[:, 64:128], finish[:, 0:64])
        middle = (begin + finish - 1) >> 1
        lower = jnp.zeros_like(middle)
        upper = jnp.full_like(middle, total_blocks)
        for k in range(bounds_ref.shape[0]):
            bound = bounds_ref[k]
            before = bound <= middle
            lower = jnp.maximum(lower, jnp.where(before, bound, 0))
            upper = jnp.minimum(upper, jnp.where(before, total_blocks, bound))
        inner = (jnp.maximum(begin, lower) <= block) & (block < jnp.minimum(finish, upper))
        msg_ref[s, :, 0:64] = jnp.where(inner, peak_ref[:, 64 * s : 64 * s + 64], 0.0)

    sends = []
    for c in range(2):
        for s in range(8):
            for k in range(2):
                local = CORE_SLOTS[c][s] == 2
                if local and k == c:
                    continue
                shift = shifts[CORE_SLOTS[c][s]]
                copy = remote(
                    msg_ref.at[s], msg_in.at[2 * (shift + 4) + c], m_send.at[2 * s + k],
                    m_recv.at[2 * (shift + 4) + c], (me + shift, k),
                )
                condition = (core == c) & inside(shift)
                when(condition, copy.start)
                sends.append((condition, copy))

    best = jnp.where(core == 0, msg_ref[2], msg_ref[1])
    for c in range(2):
        for o in range(-4 + c, 4 + c):
            index = 2 * (o + 4) + c
            condition = (core == 1 - c) if o == 0 else inside(-o)
            copy = remote(msg_ref.at[0], msg_in.at[index], m_send.at[0], m_recv.at[index], sib)
            when(condition, copy.wait_recv)
            best = jnp.maximum(best, jnp.where(condition, msg_in[index], 0.0))
    pow_copy.wait_recv()
    power = pow_ref[...] + pow_other[...]
    result = jnp.sqrt(best / (power / (2.0 * half) + 1e-05))
    out_ref[...] = result[0:5, 0:64]

    for copy in g_copies + [shuffle_copy, env_copy, mom_copy, pow_copy] + partials:
        copy.wait_send()
    finish_hops()
    for condition, copy in sends:
        when(condition, copy.wait_send)


def shards(genotypes, phenotypes, environment, shuffles, window_start, window_end, chrom_bounds):
    snps, half = genotypes.shape
    genes = phenotypes.shape[0]
    labels = shuffles.shape[0] + 1
    vmem = pl.BlockSpec(memory_space=pltpu.VMEM)

    f32, bf16, i32 = jnp.float32, jnp.bfloat16, jnp.int32
    dma = pltpu.SemaphoreType.DMA
    shape = jax.ShapeDtypeStruct
    anywhere = pl.BlockSpec(memory_space=pl.ANY)
    smem = pl.BlockSpec(memory_space=pltpu.SMEM)
    weights = environment.reshape(-1, 128)
    lines = half // 128
    return pl.pallas_call(
        scan_kernel,
        name="scan",
        out_shape=shape((labels, genes), f32),
        in_specs=[smem] + [vmem] * 4 + [anywhere] * 2,
        out_specs=vmem,
        scratch_shapes=[
            pltpu.SMEM((8, 128), i32),
            pltpu.SMEM((8, 128), i32),
            pltpu.VMEM((2 * half * 4, 128), f32),
            pltpu.VMEM((4 * half + STEP, snps), bf16),
            pltpu.VMEM((9 * genes, half), bf16),
            pltpu.VMEM((snps, half), bf16),
            pltpu.VMEM((snps, half), bf16),
            pltpu.VMEM((labels - 1, half), i32),
            pltpu.VMEM((lines, 128), f32),
            pltpu.VMEM(((labels - 1) * lines, 128), i32),
            pltpu.VMEM((snps, 128), f32),
            pltpu.VMEM((snps, 128), f32),
            pltpu.VMEM((snps, 128), f32),
            pltpu.VMEM((8, snps), f32),
            pltpu.VMEM((8, 128), f32),
            pltpu.VMEM((8, 128), f32),
            pltpu.VMEM((4 * STEP, 128), f32),
            pltpu.VMEM((4 * STEP, 128), f32),
            pltpu.VMEM((2 * labels, 256, 256), f32),
            pltpu.VMEM((2 * labels, 256, 256), f32),
            pltpu.VMEM((labels, 256, 256), f32),
            pltpu.VMEM((labels, 256, 256), f32),
            pltpu.VMEM((8, 8 * genes), f32),
            pltpu.VMEM((8, 8, 128), f32),
            pltpu.VMEM((18, 8, 128), f32),
            dma((20,)), dma((18,)), dma((4,)), dma((4,)), dma((4,)), dma((4,)),
            dma((10,)), dma((10,)), dma((16,)), dma((18,)), dma((5,)), dma((2,)),
        ],
        compiler_params=pltpu.CompilerParams(
            collective_id=0, has_side_effects=True, vmem_limit_bytes=64 * 1024 * 1024 - 65536
        ),
    )(
        chrom_bounds, shuffles, weights, window_start.reshape(-1, 128), window_end.reshape(-1, 128),
        phenotypes, genotypes,
    )


def solution(mesh):
    placed = (
        P("genome", "sample"),
        P("genome", "sample"),
        P("sample"),
        P(None, "sample"),
        P(),
        P(),
        P(),
    )
    return jax.shard_map(
        shards, mesh=mesh, in_specs=placed, out_specs=P(None, "genome"), check_vma=False
    )
```

```python
import functools

import jax
import jax.numpy as jnp
from jax import lax
from jax.experimental import pallas as pl
from jax.experimental.pallas import tpu as pltpu
from jax.sharding import PartitionSpec as P

SNP_BLOCK = 256
MESH = pl.DeviceIdType.MESH
SLOTS = (
    (-4, 3, 0, 1, 4, 2, -3, -2, -1),
    (-4, -1, 0, 1, 4, 2, -3, 3, -2),
    (-4, -1, 0, 1, 4, -2, -3, 3, 2),
    (-4, -1, 0, -3, 4, -2, 3, 2, 1),
)
CORE_SLOTS = ((0, 1, 2, 3, 5, 6, 7, 8), (1, 2, 3, 4, 5, 6, 7, 8))
STEP = 512
FAR_STEP = 1024
SPLIT = 3


def when(condition, action):
    if condition is None:
        action()
    else:
        pl.when(condition)(action)


def remote(src, dst, send, recv, target):
    return pltpu.make_async_remote_copy(
        src, dst, send, recv, device_id=target, device_id_type=MESH
    )


def residuals(source, weights, reg_ref, h_ref, k, first):
    for s in range(2):
        start = pl.multiple_of(k * 256 + s * 128, 128)
        weight = weights[pl.ds(k * 2 + s, 1), :]
        for q in range(4):
            rows = slice(q * 128, (q + 1) * 128)
            value = source[rows, pl.ds(start, 128)].astype(jnp.float32)
            value = jnp.transpose(value * (weight - reg_ref[rows, :]))
            h_ref[pl.ds((first + start) * 4 + 4 + q, 128, stride=4), :] = value


def scan_kernel(
    bounds_ref, shuffles_ref, env_ref, start_ref, end_ref, y_hbm, g_hbm,
    out_ref,
    index0, index1, h_ref, gp_ref, band_ref, g_ref, other_ref, shuffles_other, env_other, inv_ref,
    mom_ref, mom_other, reg_ref, div_ref, pow_ref, pow_other,
    stage0, stage1, near_acc, far_acc, near_in, far_in, peak_ref, msg_ref, msg_in,
    y_send, y_recv, g_send, g_recv, s_send, s_recv, p_send, p_recv, m_send, m_recv,
    local_sem, index_sem,
):
    me = lax.axis_index("genome")
    core = lax.axis_index("sample")
    indices = lax.axis_size("genome")
    sib = (me, 1 - core)
    perms, half = shuffles_ref.shape
    genes = y_hbm.shape[0]
    snps = g_hbm.shape[0]
    quarter = snps // 4
    g_loads = [
        pltpu.make_async_copy(
            g_hbm.at[pl.ds(i * quarter, quarter), :], g_ref.at[pl.ds(i * quarter, quarter), :], local_sem.at[i]
        )
        for i in range(4)
    ]
    y_load = pltpu.make_async_copy(y_hbm, band_ref.at[pl.ds(2 * genes, genes), :], local_sem.at[4])
    for copy in g_loads:
        copy.start()
    y_load.start()

    def inside(o):
        return (me + o >= 0) & (me + o < indices)

    barrier = pltpu.get_barrier_semaphore()
    pl.semaphore_signal(barrier, inc=1, device_id=sib, device_id_type=MESH)
    count = jnp.int32(1)
    for o in range(-4, 5):
        if o != 0:
            for k in range(2):
                @pl.when(inside(o))
                def _(o=o, k=k):
                    pl.semaphore_signal(barrier, inc=1, device_id=(me + o, k), device_id_type=MESH)
            count = count + jnp.where(inside(o), 2, 0)
    pl.semaphore_wait(barrier, count)

    place = lax.rem(me, 4)
    line = lax.div(me, 4)
    above, below = line > 0, line < indices // 4 - 1
    piece = genes // 2
    hops = []

    def arrival(slot, part):
        return remote(
            y_hbm.at[pl.ds(0, piece), :], band_ref.at[pl.ds(slot * genes + part * piece, piece), :],
            y_send.at[0], y_recv.at[2 * slot + part], sib,
        )

    def hop(x, link, shift, part):
        step = {"right": 1, "left": -1, "up": -4, "down": 4}[link]
        needs = set()
        if link in ("right", "left"):
            other = (x + step) % 4
            step = other - x
        else:
            other = x
            needs.add(link)
        if not 0 <= x + shift < 4:
            needs.add("up" if x + shift < 0 else "down")
        here = SLOTS[x].index(shift)
        there = SLOTS[other].index(shift - step)
        index = sum(1 for at, _ in hops if at == x)
        if shift == 0:
            source = y_hbm.at[pl.ds(part * piece, piece), :]
        else:
            source = band_ref.at[pl.ds(here * genes + part * piece, piece), :]
        copy = remote(
            source, band_ref.at[pl.ds(there * genes + part * piece, piece), :],
            y_send.at[index], y_recv.at[2 * there + part], (me + step, core),
        )
        when(rows_exist(needs), copy.start)
        hops.append((x, needs))

    def rows_exist(needs):
        if needs == {"up", "down"}:
            return above & below
        return {"up": above, "down": below}[min(needs)] if needs else None

    def finish_hops():
        for x in range(4):
            @pl.when(place == x)
            def _(x=x):
                for index, needs in enumerate([needs for at, needs in hops if at == x]):
                    copy = remote(
                        y_hbm.at[pl.ds(0, piece), :], band_ref.at[pl.ds(0, piece), :],
                        y_send.at[index], y_recv.at[0], sib,
                    )
                    when(rows_exist(needs), copy.wait_send)

    def at_place(x):
        return pl.when(place == x)

    def first_hops():
        for x in range(4):
            @at_place(x)
            def _(x=x):
                for part in range(2):
                    for link in ("right", "left", "down", "up"):
                        hop(x, link, 0, part)

    def second_hops(part):
        arrival(1, part).wait_recv()
        arrival(3, part).wait_recv()
        pl.when(above)(arrival(0, part).wait_recv)
        pl.when(below)(arrival(4, part).wait_recv)
        for x in range(4):
            @at_place(x)
            def _(x=x):
                left, right = SLOTS[x][1], SLOTS[x][3]
                if part == 0:
                    hop(x, "left", right, 0)
                else:
                    hop(x, "right", left, 1)
                if x < 3:
                    hop(x, "down", right, part)
                if x > 0:
                    hop(x, "up", left, part)
                if x == 3:
                    hop(x, "right", -4, part)
                if x == 0:
                    hop(x, "left", 4, part)

    def third_hops():
        for part in range(2):
            arrival(5, part).wait_recv()
        for x in range(4):
            @at_place(x)
            def _(x=x):
                if x < 2:
                    hop(x, "down", 2, 1)
                else:
                    hop(x, "up", -2, 1)
        inner = (place == 1) | (place == 2)
        pl.when(inner & above)(arrival(6, 0).wait_recv)
        pl.when(inner & below)(arrival(7, 0).wait_recv)
        for x in (1, 2):
            @at_place(x)
            def _(x=x):
                hop(x, "left", -3, 0)
                hop(x, "right", 3, 0)

    def last_arrivals():
        for slot in (6, 7, 8):
            for part in range(2):
                early = slot in (6, 7) and part == 0
                copy = arrival(slot, part)
                for x in range(4):
                    if early and x in (1, 2):
                        continue
                    o = SLOTS[x][slot]
                    exists = above if x + o < 0 else below
                    pl.when((place == x) & exists)(copy.wait_recv)

    shuffle_copy = remote(shuffles_ref, shuffles_other, s_send.at[0], s_recv.at[0], sib)
    env_copy = remote(env_ref, env_other, s_send.at[1], s_recv.at[1], sib)
    shuffle_copy.start()
    env_copy.start()
    first_hops()
    g_copies = [
        remote(
            g_hbm.at[pl.ds(i * quarter, quarter), :], other_ref.at[pl.ds(i * quarter, quarter), :],
            g_send.at[i], g_recv.at[i], sib,
        )
        for i in range(4)
    ]
    for copy in g_copies:
        copy.start()

    lane = lax.broadcasted_iota(jnp.int32, (64, 128), 1)

    def moments(block, _):
        first = pl.multiple_of(block * 64, 64)
        square = jnp.zeros((64, 128), jnp.float32)
        cross = square
        inter = square
        for column in range(half // 128):
            value = g_ref[pl.ds(first, 64), column * 128 : (column + 1) * 128].astype(jnp.float32)
            weight = env_ref[column : column + 1, :]
            value = value * value
            once = value * weight
            square += value
            cross += once
            inter += once * weight
        square = jnp.sum(square, axis=1, keepdims=True)
        cross = jnp.sum(cross, axis=1, keepdims=True)
        inter = jnp.sum(inter, axis=1, keepdims=True)
        mom_ref[pl.ds(first, 64), :] = jnp.where(lane == 0, square, jnp.where(lane == 1, cross, inter))
        return 0

    for copy in g_loads:
        copy.wait()
    lax.fori_loop(0, snps // 64, moments, 0)
    mom_copy = remote(mom_ref, mom_other, s_send.at[2], s_recv.at[2], sib)
    mom_copy.start()

    y_load.wait()
    power = jnp.zeros((genes, 128), jnp.float32)
    for column in range(half // 128):
        value = band_ref[2 * genes : 3 * genes, column * 128 : (column + 1) * 128].astype(jnp.float32)
        power += value * value
    power = jnp.broadcast_to(jnp.sum(power, axis=1, keepdims=True), (genes, 128))
    power = jnp.concatenate([power, power], axis=0)
    pow_ref[...] = jnp.transpose(power)[0:8, :]
    pow_copy = remote(pow_ref, pow_other, s_send.at[3], s_recv.at[3], sib)
    pow_copy.start()

    near_acc[...] = jnp.zeros_like(near_acc)
    far_acc[...] = jnp.zeros_like(far_acc)
    width = 2048
    rows = half // 128

    def located(ref, p, offset):
        total = jnp.zeros((2 * rows, 128), jnp.float32)
        for start in range(0, half, width):
            target = ref[p : p + 1, start : start + width]
            high = (target >> 7) - rows * core
            low = target & 127
            spot = lax.broadcasted_iota(jnp.int32, (1, width), 1) + (offset + start)
            hit = lax.broadcasted_iota(jnp.int32, (rows, width), 0) == high
            spot_high = (spot >> 7).astype(jnp.float32)
            spot_low = (spot & 127).astype(jnp.float32)
            lhs = jnp.concatenate(
                [jnp.where(hit, spot_high, 0.0), jnp.where(hit, spot_low, 0.0)], axis=0
            ).astype(jnp.bfloat16)
            rhs = jnp.where(
                lax.broadcasted_iota(jnp.int32, (128, width), 0) == low, 1.0, 0.0
            ).astype(jnp.bfloat16)
            total += lax.dot_general(
                lhs, rhs, (((1,), (1,)), ((), ())), preferred_element_type=jnp.float32
            )
        return total

    totals = [located(shuffles_ref, p, 0) for p in range(perms)]
    mom_copy.wait_recv()
    for q in range(4):
        lines = slice(q * 128, (q + 1) * 128)
        total = mom_ref[lines, :] + mom_other[lines, :]
        square, cross, inter = total[:, 0:1], total[:, 1:2], total[:, 2:3]
        regression = cross / square
        divisor = inter - cross * regression + 0.1 * inter
        reg_ref[lines, :] = jnp.broadcast_to(regression, (128, 128))
        div_ref[:, lines] = jnp.transpose(jnp.broadcast_to(divisor, (128, 128)))[0:8, :]

    def own_residuals(k, _):
        residuals(g_ref, env_ref, reg_ref, h_ref, k, 0)
        return 0

    lax.fori_loop(0, half // 256, own_residuals, 0)
    second_hops(0)
    shuffle_copy.wait_recv()
    for p in range(perms):
        total = totals[p] + located(shuffles_other, p, half)
        spot = (total[:rows] * 128.0 + total[rows:]).astype(jnp.int32)
        inv_ref[p * rows : (p + 1) * rows, :] = jnp.minimum(jnp.maximum(spot, 0), 2 * half - 1) * 4 + 4

    index_rows = 1024
    blocks = 4 * half // index_rows

    def index_load(ref, slot, k):
        return pltpu.make_async_copy(
            inv_ref.at[pl.ds(pl.multiple_of(k * 8, 8), 8), :], ref, index_sem.at[slot]
        )

    index_load(index0, 0, 0).start()
    index_load(index1, 1, 1).start()

    def other_residuals(k, _):
        residuals(other_ref, env_other, reg_ref, h_ref, k, half)
        return 0

    env_copy.wait_recv()
    for copy in g_copies:
        copy.wait_recv()
    lax.fori_loop(0, half // 256, other_residuals, 0)
    second_hops(1)

    def right_side(ref, first, b, count):
        return jnp.concatenate(
            [ref[pl.ds(first + 2 * b + i, count, stride=4), :] for i in range(2)], axis=1
        ).astype(jnp.bfloat16)

    run = 64
    is_upper = lax.broadcasted_iota(jnp.int32, (8, 128), 0) < 4

    def gather(stage, index, offset, first):
        for t in range(first, first + run, 2):
            row = offset + t
            upper = h_ref[pl.ds(index[row // 128, row % 128], 8), :]
            lower = h_ref[pl.ds(index[row // 128, row % 128 + 1] - 4, 8), :]
            stage[4 * t : 4 * t + 8, :] = jnp.where(is_upper, upper, lower)

    def settle(stage, n, first):
        for q in range(4):
            gp_ref[pl.ds(pl.multiple_of((n + 1) * STEP + first, run), run), 128 * q : 128 * q + 128] = (
                stage[pl.ds(4 * first + q, run, stride=4), :].astype(jnp.bfloat16)
            )

    def product(acc, rows, label, k, base, plain, blocks=(0, 1)):
        start = pl.multiple_of(k * FAR_STEP, FAR_STEP)
        for b in blocks:
            lhs = band_ref[rows[b] : rows[b] + 256, pl.ds(start, FAR_STEP)]
            if plain:
                rhs = right_side(h_ref, start * 4 + 4, b, FAR_STEP)
            else:
                rhs = gp_ref[pl.ds(pl.multiple_of(base + start, STEP), FAR_STEP), 256 * b : 256 * b + 256]
            acc[2 * label + b] += jnp.dot(lhs, rhs, preferred_element_type=jnp.float32)

    near_rows, far_rows = (0, 64), (320, 320)

    def permuted(i, _, plain=False):
        for s, (index, slot) in enumerate(((index0, 0), (index1, 1))):
            index_load(index, slot, 2 * i + s).wait()
            n = 4 * i + 2 * s
            label = lax.div(i, 2)
            k = lax.rem(2 * i + s, 4)
            base = STEP + (label - 1) * half
            for b, (stage, before) in enumerate(((stage0, stage1), (stage1, stage0))):
                product(near_acc, near_rows, label, k, base, plain, (b,))
                for first in range(0, STEP, run):
                    settle(before, n - 1 + b, first)
                    gather(stage, index, b * STEP, first)
            index_load(index, slot, lax.rem(2 * i + s + 2, blocks)).start()
        return 0

    lax.fori_loop(0, 2, functools.partial(permuted, plain=True), 0)
    lax.fori_loop(2, SPLIT, permuted, 0)
    third_hops()
    lax.fori_loop(SPLIT, blocks // 2, permuted, 0)
    for first in range(0, STEP, run):
        settle(stage1, 4 * half // STEP - 1, first)
    index_load(index0, 0, 0).wait()
    index_load(index1, 1, 1).wait()

    def last_near(k, _):
        product(near_acc, near_rows, 4, k, STEP + 3 * half, False)
        return 0

    lax.fori_loop(0, half // FAR_STEP, last_near, 0)

    partials = []
    for label in range(5):
        copy = remote(
            near_acc.at[2 * label + 1 - core], near_in.at[label], p_send.at[label], p_recv.at[label], sib
        )
        copy.start()
        partials.append(copy)
    last_arrivals()

    for label in range(5):
        def distant(k, _, label=label):
            product(far_acc, far_rows, label, k, STEP + (label - 1) * half, label == 0)
            return 0

        lax.fori_loop(0, half // FAR_STEP, distant, 0)
        copy = remote(
            far_acc.at[2 * label + 1 - core], far_in.at[label], p_send.at[5 + label], p_recv.at[5 + label], sib
        )
        copy.start()
        partials.append(copy)

    divisor = div_ref[0:1, pl.ds(pl.multiple_of(core * 256, 256), 256)]
    lanes = lax.broadcasted_iota(jnp.int32, (256, 128), 1)
    for part, (acc, arrived) in enumerate(((near_acc, near_in), (far_acc, far_in))):
        peaks = jnp.zeros((256, 128), jnp.float32)
        for label in range(5):
            partials[5 * part + label].wait_recv()
            numerator = acc[2 * label + core] + arrived[label]
            scores = numerator * numerator / divisor
            peaks = jnp.where(lanes == label, jnp.max(scores, axis=1, keepdims=True), peaks)
        peak_ref[:, 256 * part : 256 * part + 128] = jnp.transpose(peaks[0:128])[0:8, :]
        peak_ref[:, 256 * part + 128 : 256 * part + 256] = jnp.transpose(peaks[128:256])[0:8, :]
    msg_ref[...] = jnp.zeros_like(msg_ref)
    shifts = [sum(jnp.where(place == x, SLOTS[x][slot], 0) for x in range(4)) for slot in range(9)]
    block = me * (snps // SNP_BLOCK) + core
    total_blocks = indices * (snps // SNP_BLOCK)
    for s in range(8):
        shift = jnp.where(core == 0, shifts[CORE_SLOTS[0][s]], shifts[CORE_SLOTS[1][s]])
        owner = jnp.clip(me + shift, 0, indices - 1)
        odd = lax.rem(owner, 2) == 1
        begin = start_ref[pl.ds(lax.div(owner, 2), 1), :]
        finish = end_ref[pl.ds(lax.div(owner, 2), 1), :]
        begin = jnp.where(odd, begin[:, 64:128], begin[:, 0:64])
        finish = jnp.where(odd, finish[:, 64:128], finish[:, 0:64])
        middle = (begin + finish - 1) >> 1
        lower = jnp.zeros_like(middle)
        upper = jnp.full_like(middle, total_blocks)
        for k in range(bounds_ref.shape[0]):
            bound = bounds_ref[k]
            before = bound <= middle
            lower = jnp.maximum(lower, jnp.where(before, bound, 0))
            upper = jnp.minimum(upper, jnp.where(before, total_blocks, bound))
        inner = (jnp.maximum(begin, lower) <= block) & (block < jnp.minimum(finish, upper))
        msg_ref[s, :, 0:64] = jnp.where(inner, peak_ref[:, 64 * s : 64 * s + 64], 0.0)

    sends = []
    for c in range(2):
        for s in range(8):
            for k in range(2):
                local = CORE_SLOTS[c][s] == 2
                if local and k == c:
                    continue
                shift = shifts[CORE_SLOTS[c][s]]
                copy = remote(
                    msg_ref.at[s], msg_in.at[2 * (shift + 4) + c], m_send.at[2 * s + k],
                    m_recv.at[2 * (shift + 4) + c], (me + shift, k),
                )
                condition = (core == c) & inside(shift)
                when(condition, copy.start)
                sends.append((condition, copy))

    best = jnp.where(core == 0, msg_ref[2], msg_ref[1])
    for c in range(2):
        for o in range(-4 + c, 4 + c):
            index = 2 * (o + 4) + c
            condition = (core == 1 - c) if o == 0 else inside(-o)
            copy = remote(msg_ref.at[0], msg_in.at[index], m_send.at[0], m_recv.at[index], sib)
            when(condition, copy.wait_recv)
            best = jnp.maximum(best, jnp.where(condition, msg_in[index], 0.0))
    pow_copy.wait_recv()
    power = pow_ref[...] + pow_other[...]
    result = jnp.sqrt(best / (power / (2.0 * half) + 1e-05))
    out_ref[...] = result[0:5, 0:64]

    for copy in g_copies + [shuffle_copy, env_copy, mom_copy, pow_copy] + partials:
        copy.wait_send()
    finish_hops()
    for condition, copy in sends:
        when(condition, copy.wait_send)


def shards(genotypes, phenotypes, environment, shuffles, window_start, window_end, chrom_bounds):
    snps, half = genotypes.shape
    genes = phenotypes.shape[0]
    labels = shuffles.shape[0] + 1
    vmem = pl.BlockSpec(memory_space=pltpu.VMEM)

    f32, bf16, i32 = jnp.float32, jnp.bfloat16, jnp.int32
    dma = pltpu.SemaphoreType.DMA
    shape = jax.ShapeDtypeStruct
    anywhere = pl.BlockSpec(memory_space=pl.ANY)
    smem = pl.BlockSpec(memory_space=pltpu.SMEM)
    weights = environment.reshape(-1, 128)
    lines = half // 128
    return pl.pallas_call(
        scan_kernel,
        name="scan",
        out_shape=shape((labels, genes), f32),
        in_specs=[smem] + [vmem] * 4 + [anywhere] * 2,
        out_specs=vmem,
        scratch_shapes=[
            pltpu.SMEM((8, 128), i32),
            pltpu.SMEM((8, 128), i32),
            pltpu.VMEM((2 * half * 4 + 8, 128), f32),
            pltpu.VMEM((4 * half + STEP, snps), bf16),
            pltpu.VMEM((9 * genes, half), bf16),
            pltpu.VMEM((snps, half), bf16),
            pltpu.VMEM((snps, half), bf16),
            pltpu.VMEM((labels - 1, half), i32),
            pltpu.VMEM((lines, 128), f32),
            pltpu.VMEM(((labels - 1) * lines, 128), i32),
            pltpu.VMEM((snps, 128), f32),
            pltpu.VMEM((snps, 128), f32),
            pltpu.VMEM((snps, 128), f32),
            pltpu.VMEM((8, snps), f32),
            pltpu.VMEM((8, 128), f32),
            pltpu.VMEM((8, 128), f32),
            pltpu.VMEM((4 * STEP, 128), f32),
            pltpu.VMEM((4 * STEP, 128), f32),
            pltpu.VMEM((2 * labels, 256, 256), f32),
            pltpu.VMEM((2 * labels, 256, 256), f32),
            pltpu.VMEM((labels, 256, 256), f32),
            pltpu.VMEM((labels, 256, 256), f32),
            pltpu.VMEM((8, 8 * genes), f32),
            pltpu.VMEM((8, 8, 128), f32),
            pltpu.VMEM((18, 8, 128), f32),
            dma((20,)), dma((18,)), dma((4,)), dma((4,)), dma((4,)), dma((4,)),
            dma((10,)), dma((10,)), dma((16,)), dma((18,)), dma((5,)), dma((2,)),
        ],
        compiler_params=pltpu.CompilerParams(
            collective_id=0, has_side_effects=True, vmem_limit_bytes=64 * 1024 * 1024 - 65536
        ),
    )(
        chrom_bounds, shuffles, weights, window_start.reshape(-1, 128), window_end.reshape(-1, 128),
        phenotypes, genotypes,
    )


def solution(mesh):
    placed = (
        P("genome", "sample"),
        P("genome", "sample"),
        P("sample"),
        P(None, "sample"),
        P(),
        P(),
        P(),
    )
    return jax.shard_map(
        shards, mesh=mesh, in_specs=placed, out_specs=P(None, "genome"), check_vma=False
    )
```
